256 devices in a mesh: row: 16 (over x, y), col: 8 (over z), depth: 2 (over core).
Axes of the slice: x: 4, y: 4, z: 8, core: 2. Of those that a mesh axis runs over, the one named last changes fastest.
Arguments:
- covariance: float32 [3, 16, 6, 8, 256, 256], P(None, 'row', None, 'col'), may hold values from 0 to 2, as said below
Outputs:
- factored: float32 [3, 16, 6, 8, 256, 256], P(None, 'row', None, 'col', 'depth')
The draws below stay inside these ranges and needn't reach their ends.
Inputs may be any that keep to these rules, and one draw needn't show every extreme that they name: covariance is the Matern kernel of smoothness 3/2, (1 + rho) exp(-rho) with rho = sqrt(3) times the scaled distance, over 12288 points in the unit cube of 8 coordinates with length scales between 0.3 and 1.2, plus a nugget between 0.2 and 1 on the diagonal; it is symmetric positive definite.
All inputs are finite; a program needn't handle non-finite values.
Results may differ from the reference program's by a relative error of at most 0.0003.
Values sent between devices are 32-bit elements; how exact they have to be, the bound alone decides.
A program may use at most 128 MiB of HBM per device.

```python
import math
import jax
import jax.numpy as jnp
from jax import lax

ORDER = 12288
TILE = 256
DIMS = 8
STEPS = 1
N_ROW = 16
N_COL = 8


def draw_covariance(key, part):
    point_key = jax.random.fold_in(key, 11)
    scale_key = jax.random.fold_in(key, 12)
    nugget_key = jax.random.fold_in(key, 13)
    design = jax.random.uniform(point_key, (DIMS, ORDER), jnp.float32)
    scales = jnp.exp(jax.random.uniform(scale_key, (DIMS,), jnp.float32, math.log(0.3), math.log(1.2)))
    nugget = jnp.exp(jax.random.uniform(nugget_key, (), jnp.float32, math.log(0.2), math.log(1.0)))
    squared = jnp.zeros((ORDER, ORDER), jnp.float32)
    for dim_index in range(DIMS):
        offset = (design[dim_index][:, None] - design[dim_index][None, :]) / scales[dim_index]
        squared = squared + offset * offset
    radius = jnp.sqrt(squared + 1e-12) * math.sqrt(3.0)
    matrix = (1.0 + radius) * jnp.exp(-radius) + nugget * jnp.eye(ORDER, dtype=jnp.float32)
    tile_rows = ORDER // TILE // N_ROW
    tile_cols = ORDER // TILE // N_COL
    return matrix.reshape(tile_rows, N_ROW, TILE, tile_cols, N_COL, TILE).transpose(0, 1, 3, 4, 2, 5)


def setup_inputs(seed: int = 0) -> dict:
    splits = jax.random.split(jax.random.key(seed), 2)
    covariance = draw_covariance(jax.random.fold_in(splits[1], 71), 0)
    return dict(covariance=covariance)


def reference(covariance):
    panel_width = 2 * TILE
    matrix = covariance.transpose(0, 1, 4, 2, 3, 5).reshape(ORDER, ORDER)
    factors = []
    for panel_step in range(STEPS):
        first_row = panel_step * panel_width
        last_row = first_row + panel_width
        factor_lower = jnp.linalg.cholesky(matrix[first_row:last_row, first_row:last_row])
        solved = jax.scipy.linalg.solve_triangular(factor_lower, matrix[first_row:, first_row:last_row].T, lower=True).T
        factors.append(solved)
        below_rows = solved[panel_width:]
        update = jnp.dot(below_rows, below_rows.T, precision=lax.Precision.HIGHEST)
        matrix = matrix.at[last_row:, last_row:].add(-update)
    factored_width = STEPS * panel_width
    result = matrix.at[:, :factored_width].set(0.0).at[:factored_width, factored_width:].set(0.0)
    for panel_step in range(STEPS):
        first_row = panel_step * panel_width
        result = result.at[first_row:, first_row:first_row + panel_width].set(factors[panel_step])
    tile_rows = ORDER // TILE // N_ROW
    tile_cols = ORDER // TILE // N_COL
    return result.reshape(tile_rows, N_ROW, TILE, tile_cols, N_COL, TILE).transpose(0, 1, 3, 4, 2, 5)
```

```python
import functools

import jax
import jax.numpy as jnp
from jax import lax
from jax.experimental import pallas as pl
from jax.experimental.pallas import tpu as pltpu
from jax.sharding import PartitionSpec as P

TILE = 256
PANEL = 512
NB = 128
NX = NY = 4
NZ = 8
DCH = 32
CCH = 64
MESH = pl.DeviceIdType.MESH
HIGHEST = lax.Precision.HIGHEST
F32 = jnp.float32
BF16 = jnp.bfloat16


def dot_nt(a, b):
    dims = (((1,), (1,)), ((), ()))
    return lax.dot_general(a, b, dims, precision=HIGHEST, preferred_element_type=F32)


def dot_nn(a, b):
    dims = (((1,), (0,)), ((), ()))
    return lax.dot_general(a, b, dims, precision=HIGHEST, preferred_element_type=F32)


def split(x):
    hi = x.astype(BF16)
    return hi, (x - hi.astype(F32)).astype(BF16)


def dot3(a, b, dims):
    (ah, al), (bh, bl) = a, b
    dot = functools.partial(lax.dot_general, dimension_numbers=(dims, ((), ())), preferred_element_type=F32)
    return dot(ah, bh) + (dot(ah, bl) + dot(al, bh))


def lane_copy(v, k):
    return jnp.broadcast_to(v[:, k : k + 1], (8, NB))


def row_copy(v, k):
    return jnp.broadcast_to(v[k : k + 1, :], (8, NB))


def inverse_factor(rows):
    rows = list(rows)
    lane = lax.broadcasted_iota(jnp.int32, (8, NB), 1)
    sub = lax.broadcasted_iota(jnp.int32, (8, NB), 0)
    out = []
    for b in range(16):
        base = 8 * b
        cols = [[lane_copy(rows[i], base + k) for k in range(8)] for i in range(b, 16)]
        inside = (lane >= base) & (lane < base + 8)
        cur = jnp.where(inside, jnp.where(lane == sub + base, 1.0, 0.0), rows[b])
        diag = cols[0]
        scaled = jnp.zeros((8, NB), F32)
        for k in range(8):
            d = row_copy(diag[k], k)
            r = 1.0 / d
            scaled = jnp.where(sub == k, cur * lax.rsqrt(d), scaled)
            less = jnp.where(sub == k, diag[k] - 1.0, diag[k])
            for j in range(k + 1, 8):
                diag[j] = diag[j] - less * (row_copy(diag[k], j) * r)
            cur = cur - less * (row_copy(cur, k) * r)
        for i in range(b + 1, 16):
            acc = jnp.where(inside, 0.0, rows[i])
            for j in range(8):
                acc = acc - cols[i - b][j] * row_copy(cur, j)
            rows[i] = acc
        out.append(jnp.where(lane < base + 8, scaled, 0.0))
    return out


def gather_kernel(
    cov, pct_out, rp_out, w_out, pct, rp, s, w,
    d_recv, c_recv, r_recv, w_recv, d_core, c_core, r_core,
    d_send, c_send, r_send, k_send, w_send, out_sem,
):
    row = lax.axis_index("row")
    z = lax.axis_index("col")
    core = lax.axis_index("depth")
    x, y = row // NY, row % NY

    def at(xx, yy, zz):
        return {"row": lax.rem(xx + NX, NX) * NY + lax.rem(yy + NY, NY), "col": lax.rem(zz + NZ, NZ), "depth": 1}

    links = [at(x + 1, y, z), at(x - 1, y, z), at(x, y + 1, z), at(x, y - 1, z), at(x, y, z + 1), at(x, y, z - 1)]
    partner = {"row": row, "col": z, "depth": 1 - core}

    barrier = pltpu.get_barrier_semaphore()
    pl.semaphore_signal(barrier, inc=1, device_id=partner, device_id_type=MESH)

    @pl.when(core == 1)
    def _():
        for link in links:
            pl.semaphore_signal(barrier, inc=1, device_id=link, device_id_type=MESH)
        pl.semaphore_wait(barrier, 7)

    @pl.when(core == 0)
    def _():
        pl.semaphore_wait(barrier, 1)

    def remote(src, dst, send, recv, to):
        return pltpu.make_async_remote_copy(src, dst, send, recv, device_id=to, device_id_type=MESH)

    tiles = ((0, 0, 0, 0), (1, 0, 1, 0), (1, 1, 1, 1))
    per_tile = TILE // DCH

    def d_rows(t, i):
        _, _, ti, tj = tiles[t]
        return s.at[pl.ds(ti * TILE + i * DCH, DCH), pl.ds(tj * TILE, TILE)]

    def d_children(t):
        src_row, src_z, _, _ = tiles[t]
        dx, dy, dz = x, lax.rem(y - src_row + NY, NY), lax.rem(z - src_z + NZ, NZ)
        line = (dx == 0) & (dy == 0)
        return [
            (0, (dy == 0) & (dx <= 1)),
            (1, (dy == 0) & (dx == 0)),
            (2, dy <= 1),
            (3, dy == 0),
            (4, line & (dz <= 3)),
            (5, line & ((dz == 0) | (dz >= 6))),
        ], line & (dz == 0)

    def c_children(src, q):
        dx, dy = x, lax.rem(y - src + NY, NY)
        if q == 0:
            kids = [(0, (dy == 0) & (dx <= 2)), (2, dy <= 2)]
        elif q == 1:
            kids = [(1, (dy == 0) & (dx != 1)), (3, dy != 1)]
        elif q == 2:
            kids = [(2, (dx == 0) & (dy <= 2)), (0, dx <= 2)]
        else:
            kids = [(3, (dx == 0) & (dy != 1)), (1, dx != 1)]
        return kids, (dx == 0) & (dy == 0)

    def r_child(c, way):
        if way == 0:
            dz = lax.rem(z - c + NZ, NZ)
            return 4, dz <= 6, dz == 0
        dz = lax.rem(c - z + NZ, NZ)
        return 5, dz <= 6, dz == 0

    def pass_on(src, dst, here, arrived, kids, sends, recv, to_core):
        @pl.when(jnp.logical_not(here))
        def _():
            remote(dst, dst, sends(0), recv, partner).wait_recv()
        @pl.when(here)
        def _():
            for n, (link, cond) in enumerate(kids):
                @pl.when(cond)
                def _():
                    remote(src, dst, sends(n), recv, links[link]).start()
            to_core(src)
        @pl.when(jnp.logical_not(here))
        def _():
            for n, (link, cond) in enumerate(kids):
                @pl.when(cond)
                def _():
                    remote(dst, dst, sends(n), recv, links[link]).start()
            to_core(dst)

    @pl.when(core == 1)
    def _():
        for t in range(3):
            kids, here = d_children(t)
            @pl.loop(0, per_tile)
            def _(i):
                dst = d_rows(t, i)
                src = cov.at[0, 0, 0, 0, pl.ds(i * DCH, DCH), :]
                def to_core(ref):
                    remote(ref, dst, k_send.at[0, t], d_core.at[t, i], partner).start()
                pass_on(src, dst, here, None, kids, lambda n: d_send.at[t, n], d_recv.at[t, i], to_core)

        @pl.loop(0, 6)
        def _(b):
            for q in range(4):
                for src_row in range(2):
                    kids, here = c_children(src_row, q)
                    src = cov.at[0, 0, b, 0, pl.ds(q * CCH, CCH), :]
                    dst = pct.at[src_row, b, pl.ds(q * CCH, CCH), :]
                    def to_core(ref):
                        remote(ref, dst, k_send.at[1, src_row * 4 + q], c_core.at[src_row, q, b], partner).start()
                    pass_on(src, dst, here, None, kids, lambda n: c_send.at[src_row, q, n], c_recv.at[src_row, q, b], to_core)
            a, sub = b // 2, b % 2
            for way in range(2):
                for c in range(2):
                    link, cond, here = r_child(c, way)
                    rows = pl.ds(way * NB + sub * CCH, CCH)
                    src = cov.at[a, 0, 0, 0, rows, :]
                    dst = rp.at[c, a, rows, :]
                    def to_core(ref):
                        if way == 0:
                            remote(ref, dst, k_send.at[2, c], r_core.at[c, b], partner).start()
                    pass_on(src, dst, here, None, [(link, cond)], lambda n: r_send.at[c, way], r_recv.at[c, way, b], to_core)

        @pl.when((x == 0) & (y <= 1))
        def _():
            copy = pltpu.make_async_copy(cov.at[0, 0, :, 0], pct.at[y], out_sem.at[0])
            copy.start()
            copy.wait()
        @pl.when(z <= 1)
        def _():
            copy = pltpu.make_async_copy(cov.at[:, 0, 0, 0], rp.at[z], out_sem.at[0])
            copy.start()
            copy.wait()

        for t in range(3):
            kids, _ = d_children(t)
            _, _, ti, tj = tiles[t]
            whole = s.at[pl.ds(ti * TILE, TILE), pl.ds(tj * TILE, TILE)]
            for n, (link, cond) in enumerate(kids):
                @pl.when(cond)
                def _():
                    remote(whole, whole, d_send.at[t, n], d_recv.at[t, 0], partner).wait_send()
            remote(whole, whole, k_send.at[0, t], d_recv.at[t, 0], partner).wait_send()
        for src_row in range(2):
            for q in range(4):
                kids, _ = c_children(src_row, q)
                whole = pct.at[src_row, :, pl.ds(q * CCH, CCH), :]
                for n, (link, cond) in enumerate(kids):
                    @pl.when(cond)
                    def _():
                        remote(whole, whole, c_send.at[src_row, q, n], d_recv.at[0, 0], partner).wait_send()
                remote(whole, whole, k_send.at[1, src_row * 4 + q], d_recv.at[0, 0], partner).wait_send()
        for c in range(2):
            for way in range(2):
                _, cond, _ = r_child(c, way)
                whole = rp.at[c, :, pl.ds(way * NB, NB), :]
                @pl.when(cond)
                def _():
                    remote(whole, whole, r_send.at[c, way], d_recv.at[0, 0], partner).wait_send()
                if way == 0:
                    remote(whole, whole, k_send.at[2, c], d_recv.at[0, 0], partner).wait_send()
        for k in range(4):
            rows = w.at[pl.ds(k * NB, NB), :]
            remote(rows, rows, w_send.at[k], w_recv.at[k], partner).wait_recv()

    @pl.when(core == 0)
    def _():
        def wait_d(t, lo, hi):
            @pl.loop(lo, hi)
            def _(i):
                dst = d_rows(t, i)
                remote(dst, dst, d_send.at[t, 0], d_core.at[t, i], partner).wait_recv()

        w[...] = jnp.zeros_like(w)
        for k in range(4):
            o = k * NB
            e = o + NB
            if k == 0:
                wait_d(0, 0, NB // DCH)
            wk = jnp.concatenate(inverse_factor([s[o + 8 * i : o + 8 * i + 8, o:e] for i in range(16)]), axis=0)
            if k > 0:
                w[o:e, :o] = dot_nn(wk, w[o:e, :o])
            w[o:e, o:e] = wk
            rows = w.at[pl.ds(o, NB), :]
            remote(rows, rows, w_send.at[k], w_recv.at[k], partner).start()
            if k == 0:
                wait_d(0, NB // DCH, per_tile)
                wait_d(1, 0, per_tile)
                wait_d(2, 0, per_tile)
            if k < 3:
                low = dot_nt(s[e:, o:e], wk)
                for j in range(k + 1, 4):
                    f = j * NB
                    s[f:, f : f + NB] = s[f:, f : f + NB] - dot_nt(low[f - e :], low[f - e : f - e + NB])
                w[e:, :e] = w[e:, :e] - dot_nn(low, w[o:e, :e])

        @pl.loop(0, 6)
        def _(b):
            for q in range(4):
                for src_row in range(2):
                    dst = pct.at[src_row, b, pl.ds(q * CCH, CCH), :]
                    remote(dst, dst, d_send.at[0, 0], c_core.at[src_row, q, b], partner).wait_recv()
            a, sub = b // 2, b % 2
            for c in range(2):
                dst = rp.at[c, a, pl.ds(sub * CCH, CCH), :]
                remote(dst, dst, d_send.at[0, 0], r_core.at[c, b], partner).wait_recv()
        for k in range(4):
            rows = w.at[pl.ds(k * NB, NB), :]
            remote(rows, rows, w_send.at[k], w_recv.at[k], partner).wait_send()

    copies = [
        pltpu.make_async_copy(pct, pct_out, out_sem.at[0]),
        pltpu.make_async_copy(rp.at[:, :, pl.ds(core * NB, NB), :], rp_out, out_sem.at[1]),
        pltpu.make_async_copy(w, w_out, out_sem.at[2]),
    ]
    for copy in copies:
        copy.start()
    for copy in copies:
        copy.wait()


def gather(cov):
    dma = pltpu.SemaphoreType.DMA
    per_tile = TILE // DCH
    return pl.pallas_call(
        gather_kernel,
        out_shape=(
            jax.ShapeDtypeStruct((2, 6, TILE, TILE), F32),
            jax.ShapeDtypeStruct((2, 3, NB, TILE), F32),
            jax.ShapeDtypeStruct((PANEL, PANEL), F32),
        ),
        in_specs=[pl.BlockSpec(memory_space=pl.ANY)],
        out_specs=[pl.BlockSpec(memory_space=pl.ANY)] * 3,
        scratch_shapes=[
            pltpu.VMEM((2, 6, TILE, TILE), F32),
            pltpu.VMEM((2, 3, TILE, TILE), F32),
            pltpu.VMEM((PANEL, PANEL), F32),
            pltpu.VMEM((PANEL, PANEL), F32),
            dma((3, per_tile)), dma((2, 4, 6)), dma((2, 2, 6)), dma((4,)),
            dma((3, per_tile)), dma((2, 4, 6)), dma((2, 6)),
            dma((3, 6)), dma((2, 4, 2)), dma((2, 2)), dma((3, 8)), dma((4,)), dma((3,)),
        ],
        compiler_params=pltpu.CompilerParams(collective_id=0, has_side_effects=True),
        name="gather_and_factor",
    )(cov)


def update_kernel(where, cov, pct, rp, w, out, c_all, t_hi, t_lo):
    b = pl.program_id(0)
    row, z, core = where[0], where[1], where[2]
    nt, nn = ((1,), (1,)), ((1,), (0,))

    @pl.when(b == 0)
    def _():
        wsplit = split(w[...])
        rows = jnp.concatenate([rp[c].reshape(3 * NB, TILE) for c in range(2)], axis=1)
        c = dot3(split(rows), wsplit, nt)
        c_all[...] = c
        hi, lo = split(dot3(split(c), wsplit, nn))
        t_hi[...] = hi
        t_lo[...] = lo

    cols = jnp.concatenate([pct[0, 0], pct[1, 0]], axis=0)
    old = cov[:, 0, 0, 0].reshape(3 * NB, TILE)
    new = old - dot3((t_hi[...], t_lo[...]), split(cols), nn)
    sub = lax.broadcasted_iota(jnp.int32, (3 * NB, TILE), 0)
    lane = lax.broadcasted_iota(jnp.int32, (3 * NB, TILE), 1)
    top = (sub < NB) & (row < 2)
    out[...] = jnp.where(top, 0.0, new).reshape(3, 1, 1, 1, NB, TILE)

    @pl.when((b == 0) & (z < 2))
    def _():
        mine = jnp.where(z == 0, c_all[:, :TILE], c_all[:, TILE:])
        above = top & (row * TILE + core * NB + sub < z * TILE + lane)
        out[...] = jnp.where(above, 0.0, mine).reshape(3, 1, 1, 1, NB, TILE)


def update(where, cov, pct, rp, w):
    grid_spec = pltpu.PrefetchScalarGridSpec(
        num_scalar_prefetch=1,
        grid=(6,),
        in_specs=[
            pl.BlockSpec((3, 1, 1, 1, NB, TILE), lambda b, p: (0, 0, b, 0, p[2], 0)),
            pl.BlockSpec((2, 1, TILE, TILE), lambda b, p: (0, b, 0, 0)),
            pl.BlockSpec((2, 3, NB, TILE), lambda b, p: (0, 0, 0, 0)),
            pl.BlockSpec((PANEL, PANEL), lambda b, p: (0, 0)),
        ],
        out_specs=pl.BlockSpec((3, 1, 1, 1, NB, TILE), lambda b, p: (0, 0, b, 0, 0, 0)),
        scratch_shapes=[
            pltpu.VMEM((3 * NB, PANEL), F32),
            pltpu.VMEM((3 * NB, PANEL), BF16),
            pltpu.VMEM((3 * NB, PANEL), BF16),
        ],
    )
    return pl.pallas_call(
        update_kernel,
        out_shape=jax.ShapeDtypeStruct((3, 1, 6, 1, NB, TILE), F32),
        grid_spec=grid_spec,
        name="update",
    )(where, cov, pct, rp, w)


def on_device(covariance):
    where = jnp.stack([lax.axis_index("row"), lax.axis_index("col"), lax.axis_index("depth")])
    pct, rp, w = gather(covariance)
    return update(where, covariance, pct, rp, w)


def solution(mesh):
    return jax.shard_map(
        on_device,
        mesh=mesh,
        in_specs=(P(None, "row", None, "col", None, None),),
        out_specs=P(None, "row", None, "col", "depth", None),
        check_vma=False,
    )
```

```python
import functools

import jax
import jax.numpy as jnp
from jax import lax
from jax.experimental import pallas as pl
from jax.experimental.pallas import tpu as pltpu
from jax.sharding import PartitionSpec as P

TILE = 256
PANEL = 512
NB = 128
NX = NY = 4
NZ = 8
CCH = 32
TURNS = 6 * (TILE // 4 // CCH) + 2 * 7
MESH = pl.DeviceIdType.MESH
HIGHEST = lax.Precision.HIGHEST
F32 = jnp.float32
BF16 = jnp.bfloat16


def dot_nt(a, b):
    dims = (((1,), (1,)), ((), ()))
    return lax.dot_general(a, b, dims, precision=HIGHEST, preferred_element_type=F32)


def dot_nn(a, b):
    dims = (((1,), (0,)), ((), ()))
    return lax.dot_general(a, b, dims, precision=HIGHEST, preferred_element_type=F32)


def split(x):
    hi = x.astype(BF16)
    return hi, (x - hi.astype(F32)).astype(BF16)


def dot3(a, b, dims):
    (ah, al), (bh, bl) = a, b
    dot = functools.partial(lax.dot_general, dimension_numbers=(dims, ((), ())), preferred_element_type=F32)
    return dot(ah, bh) + (dot(ah, bl) + dot(al, bh))


def lane_copy(v, k):
    return jnp.broadcast_to(v[:, k : k + 1], (8, NB))


def row_copy(v, k):
    return jnp.broadcast_to(v[k : k + 1, :], (8, NB))


def inverse_factor(rows):
    rows = list(rows)
    lane = lax.broadcasted_iota(jnp.int32, (8, NB), 1)
    sub = lax.broadcasted_iota(jnp.int32, (8, NB), 0)
    out = []
    for b in range(16):
        base = 8 * b
        cols = [[lane_copy(rows[i], base + k) for k in range(8)] for i in range(b, 16)]
        inside = (lane >= base) & (lane < base + 8)
        cur = jnp.where(inside, jnp.where(lane == sub + base, 1.0, 0.0), rows[b])
        diag = cols[0]
        scaled = jnp.zeros((8, NB), F32)
        for k in range(8):
            d = row_copy(diag[k], k)
            r = 1.0 / d
            scaled = jnp.where(sub == k, cur * lax.rsqrt(d), scaled)
            less = jnp.where(sub == k, diag[k] - 1.0, diag[k])
            for j in range(k + 1, 8):
                diag[j] = diag[j] - less * (row_copy(diag[k], j) * r)
            cur = cur - less * (row_copy(cur, k) * r)
        for i in range(b + 1, 16):
            acc = jnp.where(inside, 0.0, rows[i])
            for j in range(8):
                acc = acc - cols[i - b][j] * row_copy(cur, j)
            rows[i] = acc
        out.append(jnp.where(lane < base + 8, scaled, 0.0))
    return out


def gather_kernel(
    cov, pct_out, rp_out, w_out, pct, rp, s, w,
    b_recv, d_recv, c_recv, r_recv, w_recv, d_core, c_core, r_core,
    b_send, d_send, c_send, r_send, k_send, w_send, out_sem,
):
    row = lax.axis_index("row")
    z = lax.axis_index("col")
    core = lax.axis_index("depth")
    x, y = row // NY, row % NY

    def at(xx, yy, zz, cc):
        return {"row": lax.rem(xx + NX, NX) * NY + lax.rem(yy + NY, NY), "col": lax.rem(zz + NZ, NZ), "depth": cc}

    def remote(src, dst, send, recv, to):
        return pltpu.make_async_remote_copy(src, dst, send, recv, device_id=to, device_id_type=MESH)

    partner = {"row": row, "col": z, "depth": 1 - core}
    links = [
        at(x + 1, y, z, 1), at(x - 1, y, z, 1), at(x, y + 1, z, 1),
        at(x, y - 1, z, 1), at(x, y, z + 1, 1), at(x, y, z - 1, 1),
    ]
    on_z = (row == 0) & (z == 0)
    on_y = row == 0
    on_x = x == 0
    z_kids = [at(x, y, z + n, 0) for n in (4, 5, 3, 6, 2, 7, 1)]
    y_kids = [at(x, y + n, z, 0) for n in (2, 1, 3)]
    x_kids = [at(x + n, y, z, 0) for n in (2, 1, 3)]
    trees = [(on_z, z_kids), (on_y, y_kids), (on_x, x_kids)]

    barrier = pltpu.get_barrier_semaphore()
    pl.semaphore_signal(barrier, inc=1, device_id=partner, device_id_type=MESH)

    @pl.when(core == 1)
    def _():
        for link in links:
            pl.semaphore_signal(barrier, inc=1, device_id=link, device_id_type=MESH)
        pl.semaphore_wait(barrier, 7)

    @pl.when(core == 0)
    def _():
        @pl.when(jnp.logical_not(on_x))
        def _():
            pl.semaphore_signal(barrier, inc=1, device_id=at(0 * x, y, z, 0), device_id_type=MESH)
        @pl.when(on_x & jnp.logical_not(on_y))
        def _():
            pl.semaphore_signal(barrier, inc=1, device_id=at(x, 0 * y, z, 0), device_id_type=MESH)
        @pl.when(on_y & (z != 0))
        def _():
            pl.semaphore_signal(barrier, inc=1, device_id=at(x, y, 0 * z, 0), device_id_type=MESH)
        pl.semaphore_wait(barrier, 1 + sum(cond.astype(jnp.int32) * len(kids) for cond, kids in trees))

    blocks = [(i, j) for i in range(1, 4) for j in range(i + 1)]

    def d_place(n):
        i, j = blocks[n]
        return s.at[pl.ds(i * NB, NB), pl.ds(j * NB, NB)]

    def d_tree(n):
        i, j = blocks[n]
        src_row, src_z = i // 2, j // 2
        dx, dy, dz = x, lax.rem(y - src_row + NY, NY), lax.rem(z - src_z + NZ, NZ)
        line = (dx == 0) & (dy == 0)
        kids = [
            (4, line & (dz <= 3)),
            (5, line & ((dz == 0) | (dz >= 6))),
            (0, (dy == 0) & (dx <= 1)),
            (1, (dy == 0) & (dx == 0)),
            (2, dy <= 1),
            (3, dy == 0),
        ]
        hops = jnp.minimum(dz, NZ - dz) + jnp.minimum(dx, NX - dx) + jnp.minimum(dy, NY - dy)
        return kids, line & (dz == 0), hops

    def c_tree(src, q):
        dx, dy = x, lax.rem(y - src + NY, NY)
        bx, by = lax.rem(NX - dx, NX), lax.rem(NY - dy, NY)
        if q == 0:
            return [(0, (dy == 0) & (dx <= 2)), (2, dy <= 2)], dx + dy
        if q == 1:
            return [(1, (dy == 0) & (bx <= 2)), (3, by <= 2)], bx + by
        if q == 2:
            return [(2, (dx == 0) & (dy <= 2)), (0, dx <= 2)], dx + dy
        return [(3, (dx == 0) & (by <= 2)), (1, bx <= 2)], bx + by

    def r_tree(c, way):
        hops = lax.rem((z - c if way == 0 else c - z) + NZ, NZ)
        return [(4 + way, hops <= 6)], hops

    def pass_on(live, src, dst, here, kids, sends, recv, to_core):
        def forward(ref):
            for n, (link, cond) in enumerate(kids):
                @pl.when(cond)
                def _():
                    remote(ref, dst, sends(n), recv, links[link]).start()
            to_core(ref)

        @pl.when(live & here)
        def _():
            forward(src)

        @pl.when(live & jnp.logical_not(here))
        def _():
            remote(dst, dst, sends(0), recv, partner).wait_recv()
            forward(dst)

    n_c = TILE // 4 // CCH * 6
    n_r = NB // CCH * 3

    @pl.when(core == 1)
    def _():
        @pl.loop(0, TURNS)
        def _(g):
            for n, (bi, bj) in enumerate(blocks):
                kids, here, hops = d_tree(n)
                src = cov.at[0, 0, 0, 0, pl.ds(bi % 2 * NB, NB), pl.ds(bj % 2 * NB, NB)]
                dst = d_place(n)
                def to_core(ref):
                    remote(ref, dst, k_send.at[0, n], d_core.at[n], partner).start()
                pass_on(g == n // 2 + 2 * hops, src, dst, here, kids, lambda m: d_send.at[n, m], d_recv.at[n], to_core)
            for q in range(4):
                for src_row in range(2):
                    kids, hops = c_tree(src_row, q)
                    i = g - 2 * hops
                    live = (i >= 0) & (i < n_c)
                    i = jnp.clip(i, 0, n_c - 1)
                    per = n_c // 6
                    b = i // per
                    rows = pl.ds(pl.multiple_of(q * (TILE // 4) + i % per * CCH, CCH), CCH)
                    src = cov.at[0, 0, b, 0, rows, :]
                    dst = pct.at[src_row, b, rows, :]
                    def to_core(ref):
                        remote(ref, dst, k_send.at[1, src_row * 4 + q], c_core.at[src_row, q, i], partner).start()
                    pass_on(live, src, dst, hops == 0, kids, lambda m: c_send.at[src_row, q, m], c_recv.at[src_row, q, i], to_core)
            for way in range(2):
                for c in range(2):
                    kids, hops = r_tree(c, way)
                    i = g - 2 * hops
                    live = (i >= 0) & (i < n_r)
                    i = jnp.clip(i, 0, n_r - 1)
                    per = n_r // 3
                    a = i // per
                    rows = pl.ds(pl.multiple_of(way * NB + i % per * CCH, CCH), CCH)
                    src = cov.at[a, 0, 0, 0, rows, :]
                    dst = rp.at[c, a, rows, :]
                    def to_core(ref):
                        if way == 0:
                            remote(ref, dst, k_send.at[2, c], r_core.at[c, i], partner).start()
                    pass_on(live, src, dst, hops == 0, kids, lambda m: r_send.at[c, way], r_recv.at[c, way, i], to_core)

        @pl.when((x == 0) & (y <= 1))
        def _():
            copy = pltpu.make_async_copy(cov.at[0, 0, :, 0], pct.at[y], out_sem.at[0])
            copy.start()
            copy.wait()
        @pl.when(z <= 1)
        def _():
            copy = pltpu.make_async_copy(cov.at[:, 0, 0, 0], rp.at[z], out_sem.at[0])
            copy.start()
            copy.wait()

        def left(whole, send):
            remote(whole, whole, send, d_recv.at[0], partner).wait_send()
        for n in range(len(blocks)):
            kids, _, _ = d_tree(n)
            for m, (_, cond) in enumerate(kids):
                @pl.when(cond)
                def _():
                    left(d_place(n), d_send.at[n, m])
            left(d_place(n), k_send.at[0, n])
        for src_row in range(2):
            for q in range(4):
                kids, _ = c_tree(src_row, q)
                whole = pct.at[src_row, :, pl.ds(q * (TILE // 4), TILE // 4), :]
                for m, (_, cond) in enumerate(kids):
                    @pl.when(cond)
                    def _():
                        left(whole, c_send.at[src_row, q, m])
                left(whole, k_send.at[1, src_row * 4 + q])
        for c in range(2):
            for way in range(2):
                kids, _ = r_tree(c, way)
                whole = rp.at[c, :, pl.ds(way * NB, NB), :]
                @pl.when(kids[0][1])
                def _():
                    left(whole, r_send.at[c, way])
                if way == 0:
                    left(whole, k_send.at[2, c])
        for k in range(4):
            rows = w.at[pl.ds(k * NB, NB), :]
            remote(rows, rows, w_send.at[k], w_recv.at[k], partner).wait_recv()

    @pl.when(core == 0)
    def _():
        first = s.at[pl.ds(0, NB), pl.ds(0, NB)]

        @pl.when(on_z)
        def _():
            copy = pltpu.make_async_copy(cov.at[0, 0, 0, 0, pl.ds(0, NB), pl.ds(0, NB)], first, out_sem.at[0])
            copy.start()
            copy.wait()
        @pl.when(jnp.logical_not(on_z))
        def _():
            remote(first, first, b_send.at[0], b_recv, partner).wait_recv()
        slot = 0
        for cond, kids in trees:
            @pl.when(cond)
            def _():
                for n, kid in enumerate(kids):
                    remote(first, first, b_send.at[slot + n], b_recv, kid).start()
            slot += len(kids)

        def block(i, j):
            return s[i * NB : (i + 1) * NB, j * NB : (j + 1) * NB]

        def wait_row(i):
            for n, at_n in enumerate(blocks):
                if at_n[0] == i:
                    remote(d_place(n), d_place(n), b_send.at[0], d_core.at[n], partner).wait_recv()

        w[...] = jnp.zeros_like(w)
        low = {}
        inv = {}
        for k in range(4):
            o = k * NB
            e = o + NB
            piv = block(k, k)
            if k > 0:
                low[k, k - 1] = dot_nt(low.pop((k, "left")), inv[k - 1])
                for j in range(k):
                    piv = piv - dot_nt(low[k, j], low[k, j])
                lk = jnp.concatenate([low[k, j] for j in range(k)], axis=1)
                mk = dot_nn(lk, w[:o, :o])
            wk = jnp.concatenate(inverse_factor([piv[8 * i : 8 * i + 8] for i in range(16)]), axis=0)
            inv[k] = wk
            if k > 0:
                w[o:e, :o] = -dot_nn(wk, mk)
            w[o:e, o:e] = wk
            rows = w.at[pl.ds(o, NB), :]
            remote(rows, rows, w_send.at[k], w_recv.at[k], partner).start()
            if k < 3:
                wait_row(k + 1)
                for j in range(k + 1):
                    rest = block(k + 1, j)
                    for i in range(j):
                        rest = rest - dot_nt(low[k + 1, i], low[j, i])
                    if j == k:
                        low[k + 1, "left"] = rest
                    else:
                        low[k + 1, j] = dot_nt(rest, inv[j])

        @pl.loop(0, n_c)
        def _(i):
            per = n_c // 6
            for q in range(4):
                rows = pl.ds(pl.multiple_of(q * (TILE // 4) + i % per * CCH, CCH), CCH)
                for src_row in range(2):
                    dst = pct.at[src_row, i // per, rows, :]
                    remote(dst, dst, b_send.at[0], c_core.at[src_row, q, i], partner).wait_recv()
        @pl.loop(0, n_r)
        def _(i):
            per = n_r // 3
            rows = pl.ds(pl.multiple_of(i % per * CCH, CCH), CCH)
            for c in range(2):
                dst = rp.at[c, i // per, rows, :]
                remote(dst, dst, b_send.at[0], r_core.at[c, i], partner).wait_recv()
        slot = 0
        for cond, kids in trees:
            @pl.when(cond)
            def _():
                for n, kid in enumerate(kids):
                    remote(first, first, b_send.at[slot + n], b_recv, kid).wait_send()
            slot += len(kids)
        for k in range(4):
            rows = w.at[pl.ds(k * NB, NB), :]
            remote(rows, rows, w_send.at[k], w_recv.at[k], partner).wait_send()

    copies = [
        pltpu.make_async_copy(pct, pct_out, out_sem.at[0]),
        pltpu.make_async_copy(rp.at[:, :, pl.ds(core * NB, NB), :], rp_out, out_sem.at[1]),
        pltpu.make_async_copy(w, w_out, out_sem.at[2]),
    ]
    for copy in copies:
        copy.start()
    for copy in copies:
        copy.wait()


def gather(cov):
    dma = pltpu.SemaphoreType.DMA
    n_c = TILE // 4 // CCH * 6
    n_r = NB // CCH * 3
    return pl.pallas_call(
        gather_kernel,
        out_shape=(
            jax.ShapeDtypeStruct((2, 6, TILE, TILE), F32),
            jax.ShapeDtypeStruct((2, 3, NB, TILE), F32),
            jax.ShapeDtypeStruct((PANEL, PANEL), F32),
        ),
        in_specs=[pl.BlockSpec(memory_space=pl.ANY)],
        out_specs=[pl.BlockSpec(memory_space=pl.ANY)] * 3,
        scratch_shapes=[
            pltpu.VMEM((2, 6, TILE, TILE), F32),
            pltpu.VMEM((2, 3, TILE, TILE), F32),
            pltpu.VMEM((PANEL, PANEL), F32),
            pltpu.VMEM((PANEL, PANEL), F32),
            dma, dma((9,)), dma((2, 4, n_c)), dma((2, 2, n_r)), dma((4,)),
            dma((9,)), dma((2, 4, n_c)), dma((2, n_r)),
            dma((13,)), dma((9, 6)), dma((2, 4, 2)), dma((2, 2)), dma((3, 9)), dma((4,)), dma((3,)),
        ],
        compiler_params=pltpu.CompilerParams(collective_id=0, has_side_effects=True),
        name="gather_and_factor",
    )(cov)


def update_kernel(where, cov, pct, rp, w, out, c_all, t_hi, t_lo):
    b = pl.program_id(0)
    row, z, core = where[0], where[1], where[2]
    nt, nn = ((1,), (1,)), ((1,), (0,))

    @pl.when(b == 0)
    def _():
        wsplit = split(w[...])
        rows = jnp.concatenate([rp[c].reshape(3 * NB, TILE) for c in range(2)], axis=1)
        c = dot3(split(rows), wsplit, nt)
        c_all[...] = c
        hi, lo = split(dot3(split(c), wsplit, nn))
        t_hi[...] = hi
        t_lo[...] = lo

    cols = jnp.concatenate([pct[0, 0], pct[1, 0]], axis=0)
    old = cov[:, 0, 0, 0].reshape(3 * NB, TILE)
    new = old - dot3((t_hi[...], t_lo[...]), split(cols), nn)
    sub = lax.broadcasted_iota(jnp.int32, (3 * NB, TILE), 0)
    lane = lax.broadcasted_iota(jnp.int32, (3 * NB, TILE), 1)
    top = (sub < NB) & (row < 2)
    out[...] = jnp.where(top, 0.0, new).reshape(3, 1, 1, 1, NB, TILE)

    @pl.when((b == 0) & (z < 2))
    def _():
        mine = jnp.where(z == 0, c_all[:, :TILE], c_all[:, TILE:])
        above = top & (row * TILE + core * NB + sub < z * TILE + lane)
        out[...] = jnp.where(above, 0.0, mine).reshape(3, 1, 1, 1, NB, TILE)


def update(where, cov, pct, rp, w):
    grid_spec = pltpu.PrefetchScalarGridSpec(
        num_scalar_prefetch=1,
        grid=(6,),
        in_specs=[
            pl.BlockSpec((3, 1, 1, 1, NB, TILE), lambda b, p: (0, 0, b, 0, p[2], 0)),
            pl.BlockSpec((2, 1, TILE, TILE), lambda b, p: (0, b, 0, 0)),
            pl.BlockSpec((2, 3, NB, TILE), lambda b, p: (0, 0, 0, 0)),
            pl.BlockSpec((PANEL, PANEL), lambda b, p: (0, 0)),
        ],
        out_specs=pl.BlockSpec((3, 1, 1, 1, NB, TILE), lambda b, p: (0, 0, b, 0, 0, 0)),
        scratch_shapes=[
            pltpu.VMEM((3 * NB, PANEL), F32),
            pltpu.VMEM((3 * NB, PANEL), BF16),
            pltpu.VMEM((3 * NB, PANEL), BF16),
        ],
    )
    return pl.pallas_call(
        update_kernel,
        out_shape=jax.ShapeDtypeStruct((3, 1, 6, 1, NB, TILE), F32),
        grid_spec=grid_spec,
        name="update",
    )(where, cov, pct, rp, w)


def on_device(covariance):
    where = jnp.stack([lax.axis_index("row"), lax.axis_index("col"), lax.axis_index("depth")])
    pct, rp, w = gather(covariance)
    return update(where, covariance, pct, rp, w)


def solution(mesh):
    return jax.shard_map(
        on_device,
        mesh=mesh,
        in_specs=(P(None, "row", None, "col", None, None),),
        out_specs=P(None, "row", None, "col", "depth", None),
        check_vma=False,
    )
```

```python
import functools

import jax
import jax.numpy as jnp
from jax import lax
from jax.experimental import pallas as pl
from jax.experimental.pallas import tpu as pltpu
from jax.sharding import PartitionSpec as P

TILE = 256
PANEL = 512
NB = 128
NX = NY = 4
NZ = 8
CCH = 32
LAG = 2
TURNS = 6 * (TILE // 4 // CCH) + LAG * 7
HALF = TILE // 2
MESH = pl.DeviceIdType.MESH
HIGHEST = lax.Precision.HIGHEST
F32 = jnp.float32
BF16 = jnp.bfloat16


def dot_nt(a, b):
    dims = (((1,), (1,)), ((), ()))
    return lax.dot_general(a, b, dims, precision=HIGHEST, preferred_element_type=F32)


def dot_nn(a, b):
    dims = (((1,), (0,)), ((), ()))
    return lax.dot_general(a, b, dims, precision=HIGHEST, preferred_element_type=F32)


def split(x):
    hi = x.astype(BF16)
    return hi, (x - hi.astype(F32)).astype(BF16)


def dot3(a, b, dims):
    (ah, al), (bh, bl) = a, b
    dot = functools.partial(lax.dot_general, dimension_numbers=(dims, ((), ())), preferred_element_type=F32)
    return dot(ah, bh) + (dot(ah, bl) + dot(al, bh))


def lane_copy(v, k):
    return jnp.broadcast_to(v[:, k : k + 1], (8, NB))


def row_copy(v, k):
    return jnp.broadcast_to(v[k : k + 1, :], (8, NB))


def inverse_factor(rows):
    rows = list(rows)
    lane = lax.broadcasted_iota(jnp.int32, (8, NB), 1)
    sub = lax.broadcasted_iota(jnp.int32, (8, NB), 0)
    out = []
    for b in range(16):
        base = 8 * b
        cols = [[lane_copy(rows[i], base + k) for k in range(8)] for i in range(b, 16)]
        inside = (lane >= base) & (lane < base + 8)
        cur = jnp.where(inside, jnp.where(lane == sub + base, 1.0, 0.0), rows[b])
        diag = cols[0]
        scaled = jnp.zeros((8, NB), F32)
        for k in range(8):
            d = row_copy(diag[k], k)
            r = 1.0 / d
            scaled = jnp.where(sub == k, cur * lax.rsqrt(d), scaled)
            less = jnp.where(sub == k, diag[k] - 1.0, diag[k])
            for j in range(k + 1, 8):
                diag[j] = diag[j] - less * (row_copy(diag[k], j) * r)
            cur = cur - less * (row_copy(cur, k) * r)
        for i in range(b + 1, 16):
            acc = jnp.where(inside, 0.0, rows[i])
            for j in range(8):
                acc = acc - cols[i - b][j] * row_copy(cur, j)
            rows[i] = acc
        out.append(jnp.where(lane < base + 8, scaled, 0.0))
    return out


def panel_kernel(
    cov, out, pct, rp, s, w, m3, mine, c_all, t_hi, t_lo,
    b_recv, d_recv, c_recv, r_recv, p_recv, d_core, c_core, r_core, p_core,
    b_send, d_send, c_send, r_send, k_send, p_send, in_sem, out_sem,
):
    row = lax.axis_index("row")
    z = lax.axis_index("col")
    core = lax.axis_index("depth")
    x, y = row // NY, row % NY

    def at(xx, yy, zz, cc):
        return {"row": lax.rem(xx + NX, NX) * NY + lax.rem(yy + NY, NY), "col": lax.rem(zz + NZ, NZ), "depth": cc}

    def remote(src, dst, send, recv, to):
        return pltpu.make_async_remote_copy(src, dst, send, recv, device_id=to, device_id_type=MESH)

    partner = {"row": row, "col": z, "depth": 1 - core}
    links = [
        at(x + 1, y, z, 1), at(x - 1, y, z, 1), at(x, y + 1, z, 1),
        at(x, y - 1, z, 1), at(x, y, z + 1, 1), at(x, y, z - 1, 1),
    ]
    z_kids = [at(x, y, z + n, 0) for n in (4, 5, 3, 6, 2, 7, 1)]
    y_kids = [at(x, y + n, z, 0) for n in (2, 1, 3)]
    x_kids = [at(x + n, y, z, 0) for n in (2, 1, 3)]
    hub = row == 0
    trees = [(hub & (z == 0), z_kids), (hub, y_kids), (x == 0, x_kids)]

    own = [
        pltpu.make_async_copy(cov.at[:, 0, b, 0, pl.ds(core * HALF, HALF), :], mine.at[:, b], in_sem.at[b])
        for b in range(6)
    ]

    barrier = pltpu.get_barrier_semaphore()
    pl.semaphore_signal(barrier, inc=1, device_id=partner, device_id_type=MESH)

    @pl.when(core == 1)
    def _():
        for link in links:
            pl.semaphore_signal(barrier, inc=1, device_id=link, device_id_type=MESH)
        pl.semaphore_wait(barrier, 7)

    @pl.when(core == 0)
    def _():
        @pl.when(x != 0)
        def _():
            pl.semaphore_signal(barrier, inc=1, device_id=at(0 * x, y, z, 0), device_id_type=MESH)
        @pl.when((x == 0) & (y != 0))
        def _():
            pl.semaphore_signal(barrier, inc=1, device_id=at(x, 0 * y, z, 0), device_id_type=MESH)
        @pl.when(hub & (z != 0))
        def _():
            pl.semaphore_signal(barrier, inc=1, device_id=at(x, y, 0 * z, 0), device_id_type=MESH)
        pl.semaphore_wait(barrier, 1 + sum(cond.astype(jnp.int32) * len(kids) for cond, kids in trees))

    blocks = [(i, j) for i in range(1, 4) for j in range(i + 1)]

    def d_place(n):
        i, j = blocks[n]
        return s.at[pl.ds(i * NB, NB), pl.ds(j * NB, NB)]

    def d_tree(n):
        i, j = blocks[n]
        src_row, src_z = i // 2, j // 2
        dz = lax.rem(z - src_z + NZ, NZ)
        kids = [(4, hub & (dz <= 3)), (5, hub & ((dz == 0) | (dz >= 6)))]
        hops = jnp.minimum(dz, NZ - dz) + jnp.where(hub, src_row, 0)
        here = (row == src_row) & (dz == 0)
        if src_row:
            kids.append((3, here))
        return kids, hub | here, here, hops

    def c_tree(src, q):
        dx, dy = x, lax.rem(y - src + NY, NY)
        if q % 2:
            dx, dy = lax.rem(NX - dx, NX), lax.rem(NY - dy, NY)
        if q >= 2:
            dx, dy = dy, dx
        along = (dy == 0) & (dx <= 2) | (dx == 3) & (dy >= 1)
        across = (dx >= 1) & (dy <= 2)
        hops = jnp.where((dx == 0) & (dy > 0), dy + 4, dx + dy)
        one, two = (q % 2, 2 + q % 2) if q < 2 else (2 + q % 2, q % 2)
        return [(one, along), (two, across)], hops

    def r_tree(c, way):
        hops = lax.rem((z - c if way == 0 else c - z) + NZ, NZ)
        return [(4 + way, hops <= 6)], hops

    def pass_on(live, src, dst, here, kids, sends, recv, to_core):
        def forward(ref):
            for n, (link, cond) in enumerate(kids):
                @pl.when(cond)
                def _():
                    remote(ref, dst, sends(n), recv, links[link]).start()
            to_core(ref)

        @pl.when(live & here)
        def _():
            forward(src)

        @pl.when(live & jnp.logical_not(here))
        def _():
            remote(dst, dst, sends(0), recv, partner).wait_recv()
            forward(dst)

    n_c = TILE // 4 // CCH * 6
    n_r = NB // CCH * 3

    def piece(k):
        if k == 3:
            return m3
        i = min(k, 3)
        return w.at[pl.ds(i * NB, NB), pl.ds(0, (i + 1) * NB)] if k < 3 else w.at[pl.ds(3 * NB, NB), pl.ds(3 * NB, NB)]

    def hand_out(k):
        slot = 0
        for cond, kids in trees[1:]:
            @pl.when(cond)
            def _():
                for n, kid in enumerate(kids):
                    remote(piece(k), piece(k), p_send.at[k, slot + n], p_recv.at[k], kid).start()
            slot += len(kids)
        remote(piece(k), piece(k), p_send.at[k, slot], p_core.at[k], partner).start()

    @pl.when(core == 1)
    def _():
        @pl.loop(0, TURNS)
        def _(g):
            for n, (bi, bj) in enumerate(blocks):
                kids, on_way, here, hops = d_tree(n)
                src = cov.at[0, 0, 0, 0, pl.ds(bi % 2 * NB, NB), pl.ds(bj % 2 * NB, NB)]
                dst = d_place(n)
                def to_core(ref):
                    @pl.when(hub)
                    def _():
                        remote(ref, dst, k_send.at[0, n], d_core.at[n], partner).start()
                pass_on(on_way & (g == n // 2 + LAG * hops), src, dst, here, kids, lambda m: d_send.at[n, m], d_recv.at[n], to_core)
            for q in range(4):
                for src_row in range(2):
                    kids, hops = c_tree(src_row, q)
                    i = g - LAG * hops
                    live = (i >= 0) & (i < n_c)
                    i = jnp.clip(i, 0, n_c - 1)
                    per = n_c // 6
                    b = i // per
                    rows = pl.ds(pl.multiple_of(q * (TILE // 4) + i % per * CCH, CCH), CCH)
                    src = cov.at[0, 0, b, 0, rows, :]
                    dst = pct.at[src_row, b, rows, :]
                    def to_core(ref):
                        remote(ref, dst, k_send.at[1, src_row * 4 + q], c_core.at[src_row, q, i], partner).start()
                    pass_on(live, src, dst, hops == 0, kids, lambda m: c_send.at[src_row, q, m], c_recv.at[src_row, q, i], to_core)
            for way in range(2):
                for c in range(2):
                    kids, hops = r_tree(c, way)
                    i = g - LAG * hops
                    live = (i >= 0) & (i < n_r)
                    i = jnp.clip(i, 0, n_r - 1)
                    per = n_r // 3
                    a = i // per
                    rows = pl.ds(pl.multiple_of(way * NB + i % per * CCH, CCH), CCH)
                    src = cov.at[a, 0, 0, 0, rows, :]
                    dst = rp.at[c, a, rows, :]
                    def to_core(ref):
                        if way == 0:
                            remote(ref, dst, k_send.at[2, c], r_core.at[c, i], partner).start()
                    pass_on(live, src, dst, hops == 0, kids, lambda m: r_send.at[c, way], r_recv.at[c, way, i], to_core)

        @pl.when((x == 0) & (y <= 1))
        def _():
            copy = pltpu.make_async_copy(cov.at[0, 0, :, 0], pct.at[y], out_sem.at[0])
            copy.start()
            copy.wait()
        @pl.when(z <= 1)
        def _():
            copy = pltpu.make_async_copy(cov.at[:, 0, 0, 0], rp.at[z], out_sem.at[0])
            copy.start()
            copy.wait()
        for copy in own:
            copy.start()
        for k in range(5):
            remote(piece(k), piece(k), p_send.at[0, 0], p_core.at[k], partner).wait_recv()

    @pl.when((core == 0) & jnp.logical_not(hub))
    def _():
        for copy in own:
            copy.start()
        for k in range(5):
            remote(piece(k), piece(k), p_send.at[0, 0], p_recv.at[k], partner).wait_recv()
            hand_out(k)

    @pl.when((core == 0) & hub)
    def _():
        first = s.at[pl.ds(0, NB), pl.ds(0, NB)]
        first_in = cov.at[0, 0, 0, 0, pl.ds(0, NB), pl.ds(0, NB)]

        @pl.when(z == 0)
        def _():
            for n, kid in enumerate(z_kids):
                remote(first_in, first, b_send.at[n], b_recv, kid).start()
            copy = pltpu.make_async_copy(first_in, first, out_sem.at[0])
            copy.start()
            copy.wait()
        @pl.when(z != 0)
        def _():
            remote(first, first, b_send.at[0], b_recv, partner).wait_recv()

        def block(i, j):
            return s[i * NB : (i + 1) * NB, j * NB : (j + 1) * NB]

        def wait_row(i):
            for n, at_n in enumerate(blocks):
                if at_n[0] == i:
                    remote(d_place(n), d_place(n), b_send.at[0], d_core.at[n], partner).wait_recv()

        low = {}
        inv = {}
        for k in range(4):
            o = k * NB
            piv = block(k, k)
            if k > 0:
                low[k, k - 1] = dot_nt(low.pop((k, "left")), inv[k - 1])
                for j in range(k):
                    piv = piv - dot_nt(low[k, j], low[k, j])
                mk = None
                for j in range(k):
                    part = dot_nn(low[k, j], w[j * NB : (j + 1) * NB, : (j + 1) * NB])
                    if j < k - 1:
                        part = jnp.concatenate([part, jnp.zeros((NB, (k - 1 - j) * NB), F32)], axis=1)
                    mk = part if mk is None else mk + part
                if k == 3:
                    m3[...] = mk
                    hand_out(3)
            wk = jnp.concatenate(inverse_factor([piv[8 * i : 8 * i + 8] for i in range(16)]), axis=0)
            inv[k] = wk
            if 0 < k < 3:
                w[o : o + NB, :o] = -dot_nn(wk, mk)
            w[o : o + NB, o : o + NB] = wk
            hand_out(k if k < 3 else 4)
            if k == 0:
                for copy in own:
                    copy.start()
            if k < 3:
                wait_row(k + 1)
                for j in range(k + 1):
                    rest = block(k + 1, j)
                    for i in range(j):
                        rest = rest - dot_nt(low[k + 1, i], low[j, i])
                    if j == k:
                        low[k + 1, "left"] = rest
                    else:
                        low[k + 1, j] = dot_nt(rest, inv[j])

    @pl.when(core == 0)
    def _():
        @pl.loop(0, n_c)
        def _(i):
            per = n_c // 6
            for q in range(4):
                rows = pl.ds(pl.multiple_of(q * (TILE // 4) + i % per * CCH, CCH), CCH)
                for src_row in range(2):
                    dst = pct.at[src_row, i // per, rows, :]
                    remote(dst, dst, b_send.at[0], c_core.at[src_row, q, i], partner).wait_recv()
        @pl.loop(0, n_r)
        def _(i):
            per = n_r // 3
            rows = pl.ds(pl.multiple_of(i % per * CCH, CCH), CCH)
            for c in range(2):
                dst = rp.at[c, i // per, rows, :]
                remote(dst, dst, b_send.at[0], r_core.at[c, i], partner).wait_recv()

    parts = lambda ref: split(ref)
    tri = [parts(w[j * NB : (j + 1) * NB, : (j + 1) * NB]) for j in range(3)]
    last = w[3 * NB :, 3 * NB :]
    left = dot_nn(last, m3[...])
    tri.append(parts(jnp.concatenate([-left, last], axis=1)))
    nt, nn = ((1,), (1,)), ((1,), (0,))
    rows = [rp[c, :, pl.ds(core * HALF, HALF), :].reshape(3 * HALF, TILE) for c in range(2)]
    r_hi, r_lo = split(jnp.concatenate(rows, axis=1))
    c_parts = []
    for j in range(4):
        e = (j + 1) * NB
        got = dot3((r_hi[:, :e], r_lo[:, :e]), tri[j], nt)
        c_all[:, j * NB : e] = got
        c_parts.append(split(got))
    for j in range(4):
        cols = slice(j * NB, (j + 1) * NB)
        lhs = [jnp.concatenate([c_parts[i][h] for i in range(j, 4)], axis=1) for h in range(2)]
        rhs = [jnp.concatenate([tri[i][h][:, cols] for i in range(j, 4)], axis=0) for h in range(2)]
        hi, lo = split(dot3(lhs, rhs, nn))
        t_hi[:, cols] = hi
        t_lo[:, cols] = lo

    sub = lax.broadcasted_iota(jnp.int32, (3 * HALF, TILE), 0)
    lane = lax.broadcasted_iota(jnp.int32, (3 * HALF, TILE), 1)
    top = (sub < HALF) & (row < 2)

    def put(b):
        return pltpu.make_async_copy(mine.at[:, b], out.at[:, 0, b, 0], out_sem.at[b])

    for copy in own:
        copy.wait()

    @pl.loop(0, 6)
    def _(b):
        cols = jnp.concatenate([pct[0, b], pct[1, b]], axis=0)
        old = mine[:, b].reshape(3 * HALF, TILE)
        new = old - dot3((t_hi[...], t_lo[...]), split(cols), nn)
        mine[:, b] = jnp.where(top, 0.0, new).reshape(3, HALF, TILE)

        @pl.when((b == 0) & (z < 2))
        def _():
            panel = jnp.where(z == 0, c_all[:, :TILE], c_all[:, TILE:])
            above = top & (row * TILE + core * HALF + sub < z * TILE + lane)
            mine[:, 0] = jnp.where(above, 0.0, panel).reshape(3, HALF, TILE)
        put(b).start()

    def left_for(whole, send):
        remote(whole, whole, send, p_recv.at[0], partner).wait_send()

    @pl.when(core == 1)
    def _():
        for n in range(len(blocks)):
            kids, _, _, _ = d_tree(n)
            for m, (_, cond) in enumerate(kids):
                @pl.when(cond)
                def _():
                    left_for(d_place(n), d_send.at[n, m])
            @pl.when(hub)
            def _():
                left_for(d_place(n), k_send.at[0, n])
        for src_row in range(2):
            for q in range(4):
                kids, _ = c_tree(src_row, q)
                whole = pct.at[src_row, :, pl.ds(q * (TILE // 4), TILE // 4), :]
                for m, (_, cond) in enumerate(kids):
                    @pl.when(cond)
                    def _():
                        left_for(whole, c_send.at[src_row, q, m])
                left_for(whole, k_send.at[1, src_row * 4 + q])
        for c in range(2):
            for way in range(2):
                kids, _ = r_tree(c, way)
                whole = rp.at[c, :, pl.ds(way * NB, NB), :]
                @pl.when(kids[0][1])
                def _():
                    left_for(whole, r_send.at[c, way])
                if way == 0:
                    left_for(whole, k_send.at[2, c])

    @pl.when(core == 0)
    def _():
        first = s.at[pl.ds(0, NB), pl.ds(0, NB)]
        @pl.when(trees[0][0])
        def _():
            for n in range(len(z_kids)):
                left_for(first, b_send.at[n])
        for k in range(5):
            slot = 0
            for cond, kids in trees[1:]:
                @pl.when(cond)
                def _():
                    for n in range(len(kids)):
                        left_for(piece(k), p_send.at[k, slot + n])
                slot += len(kids)
            left_for(piece(k), p_send.at[k, slot])

    @pl.loop(0, 6)
    def _(b):
        put(b).wait()


def on_device(covariance):
    dma = pltpu.SemaphoreType.DMA
    n_c = TILE // 4 // CCH * 6
    n_r = NB // CCH * 3
    return pl.pallas_call(
        panel_kernel,
        out_shape=jax.ShapeDtypeStruct((3, 1, 6, 1, HALF, TILE), F32),
        in_specs=[pl.BlockSpec(memory_space=pl.ANY)],
        out_specs=pl.BlockSpec(memory_space=pl.ANY),
        scratch_shapes=[
            pltpu.VMEM((2, 6, TILE, TILE), F32),
            pltpu.VMEM((2, 3, TILE, TILE), F32),
            pltpu.VMEM((PANEL, PANEL), F32),
            pltpu.VMEM((PANEL, PANEL), F32),
            pltpu.VMEM((NB, 3 * NB), F32),
            pltpu.VMEM((3, 6, HALF, TILE), F32),
            pltpu.VMEM((3 * HALF, PANEL), F32),
            pltpu.VMEM((3 * HALF, PANEL), BF16),
            pltpu.VMEM((3 * HALF, PANEL), BF16),
            dma, dma((9,)), dma((2, 4, n_c)), dma((2, 2, n_r)), dma((5,)),
            dma((9,)), dma((2, 4, n_c)), dma((2, n_r)), dma((5,)),
            dma((7,)), dma((9, 3)), dma((2, 4, 2)), dma((2, 2)), dma((3, 9)), dma((5, 7)), dma((6,)), dma((6,)),
        ],
        compiler_params=pltpu.CompilerParams(collective_id=0, has_side_effects=True),
        name="panel_step",
    )(covariance)


def solution(mesh):
    return jax.shard_map(
        on_device,
        mesh=mesh,
        in_specs=(P(None, "row", None, "col", None, None),),
        out_specs=P(None, "row", None, "col", "depth", None),
        check_vma=False,
    )
```

```python
import functools

import jax
import jax.numpy as jnp
from jax import lax
from jax.experimental import pallas as pl
from jax.experimental.pallas import tpu as pltpu
from jax.sharding import PartitionSpec as P

TILE = 256
PANEL = 512
NB = 128
NX = NY = 4
NZ = 8
CCH = 64
LAG = 2
TURNS = 6 * (TILE // 4 // CCH) + LAG * 7
HALF = TILE // 2
MESH = pl.DeviceIdType.MESH
HIGHEST = lax.Precision.HIGHEST
F32 = jnp.float32
BF16 = jnp.bfloat16


def dot_nt(a, b):
    dims = (((1,), (1,)), ((), ()))
    return lax.dot_general(a, b, dims, precision=HIGHEST, preferred_element_type=F32)


def dot_nn(a, b):
    dims = (((1,), (0,)), ((), ()))
    return lax.dot_general(a, b, dims, precision=HIGHEST, preferred_element_type=F32)


def split(x):
    hi = x.astype(BF16)
    return hi, (x - hi.astype(F32)).astype(BF16)


def dot3(a, b, dims):
    (ah, al), (bh, bl) = a, b
    dot = functools.partial(lax.dot_general, dimension_numbers=(dims, ((), ())), preferred_element_type=F32)
    return dot(ah, bh) + (dot(ah, bl) + dot(al, bh))


def lane_copy(v, k):
    return jnp.broadcast_to(v[:, k : k + 1], (8, NB))


def row_copy(v, k):
    return jnp.broadcast_to(v[k : k + 1, :], (8, NB))


def inverse_factor(rows):
    rows = list(rows)
    lane = lax.broadcasted_iota(jnp.int32, (8, NB), 1)
    sub = lax.broadcasted_iota(jnp.int32, (8, NB), 0)
    out = []
    for b in range(16):
        base = 8 * b
        cols = [[lane_copy(rows[i], base + k) for k in range(8)] for i in range(b, 16)]
        inside = (lane >= base) & (lane < base + 8)
        cur = jnp.where(inside, jnp.where(lane == sub + base, 1.0, 0.0), rows[b])
        diag = cols[0]
        scaled = jnp.zeros((8, NB), F32)
        for k in range(8):
            d = row_copy(diag[k], k)
            r = 1.0 / d
            scaled = jnp.where(sub == k, cur * lax.rsqrt(d), scaled)
            less = jnp.where(sub == k, diag[k] - 1.0, diag[k])
            for j in range(k + 1, 8):
                diag[j] = diag[j] - less * (row_copy(diag[k], j) * r)
            cur = cur - less * (row_copy(cur, k) * r)
        for i in range(b + 1, 16):
            acc = jnp.where(inside, 0.0, rows[i])
            for j in range(8):
                acc = acc - cols[i - b][j] * row_copy(cur, j)
            rows[i] = acc
        out.append(jnp.where(lane < base + 8, scaled, 0.0))
    return out


def panel_kernel(
    cov, out, pct, rp, s, w, mine, c_all, t_hi, t_lo,
    b_recv, d_recv, a_recv, c_recv, r_recv, p_recv, c_core, r_core, p_core,
    b_send, a_send, c_send, r_send, k_send, p_send, in_sem, out_sem, local_sem,
):
    row = lax.axis_index("row")
    z = lax.axis_index("col")
    core = lax.axis_index("depth")
    x, y = row // NY, row % NY

    def at(xx, yy, zz, cc):
        return {"row": lax.rem(xx + NX, NX) * NY + lax.rem(yy + NY, NY), "col": lax.rem(zz + NZ, NZ), "depth": cc}

    def remote(src, dst, send, recv, to):
        return pltpu.make_async_remote_copy(src, dst, send, recv, device_id=to, device_id_type=MESH)

    partner = {"row": row, "col": z, "depth": 1 - core}
    links = [
        at(x + 1, y, z, 1), at(x - 1, y, z, 1), at(x, y + 1, z, 1),
        at(x, y - 1, z, 1), at(x, y, z + 1, 1), at(x, y, z - 1, 1),
    ]
    z_kids = [at(x, y, z + n, 0) for n in (4, 5, 3, 6, 2, 7, 1)]
    y_kids = [at(x, y + n, z, 0) for n in (2, 1, 3)]
    x_kids = [at(x + n, y, z, 0) for n in (2, 1, 3)]
    hub = row == 0
    trees = [(hub & (z == 0), z_kids), (hub, y_kids), (x == 0, x_kids)]

    own = [
        pltpu.make_async_copy(cov.at[:, 0, b, 0, pl.ds(core * HALF, HALF), :], mine.at[:, b], in_sem)
        for b in range(6)
    ]

    blocks = [
        (1, 0, 1, 0), (1, 1, 3, 0), (2, 0, 0, 1), (2, 1, 1, 1), (2, 2, 0, 1),
        (3, 0, 3, 1), (3, 1, 0, 2), (3, 2, 1, 1), (3, 3, 3, 1),
    ]

    def d_place(n):
        i, j, _, _ = blocks[n]
        return s.at[pl.ds(i * NB, NB), pl.ds(j * NB, NB)]

    def d_input(n):
        i, j, _, _ = blocks[n]
        return cov.at[0, 0, 0, 0, pl.ds(i % 2 * NB, NB), pl.ds(j % 2 * NB, NB)]

    def d_roles(n):
        i, j, ax, ay = blocks[n]
        source = (x == 0) & (y == i // 2) & (z == j // 2)
        agent = (x == ax) & (y == ay) & (z == j // 2)
        return source, agent, (ax, ay) == (0, i // 2)

    hubs = [at(0 * x, 0 * y, n + 0 * z, 0) for n in (4, 5, 3, 6, 2, 7, 1, 0)]
    outs = [[n for n in range(9) if blocks[n][0] // 2 == sy and blocks[n][1] // 2 == sz and not d_roles(n)[2]] for sy, sz in ((0, 0), (1, 0), (1, 1))]
    d_rows = {1: s.at[pl.ds(0, NB), pl.ds(0, 2 * NB)], 2: s.at[pl.ds(0, NB), pl.ds(0, 3 * NB)], 3: s.at[pl.ds(0, NB), :]}

    barrier = pltpu.get_barrier_semaphore()
    pl.semaphore_signal(barrier, inc=1, device_id=partner, device_id_type=MESH)

    @pl.when(core == 1)
    def _():
        for link in links:
            pl.semaphore_signal(barrier, inc=1, device_id=link, device_id_type=MESH)
        pl.semaphore_wait(barrier, 7)

    @pl.when(core == 0)
    def _():
        @pl.when(x != 0)
        def _():
            pl.semaphore_signal(barrier, inc=1, device_id=at(0 * x, y, z, 0), device_id_type=MESH)
        @pl.when((x == 0) & (y != 0))
        def _():
            pl.semaphore_signal(barrier, inc=1, device_id=at(x, 0 * y, z, 0), device_id_type=MESH)
        @pl.when(hub & (z != 0))
        def _():
            pl.semaphore_signal(barrier, inc=1, device_id=at(x, y, 0 * z, 0), device_id_type=MESH)
        want = 1 + sum(cond.astype(jnp.int32) * len(kids) for cond, kids in trees)
        for n in range(9):
            i, j, ax, ay = blocks[n]
            source, agent, same = d_roles(n)
            @pl.when(hub)
            def _():
                to = at(0 * x + ax, 0 * y + ay, 0 * z + j // 2, 0)
                pl.semaphore_signal(barrier, inc=1, device_id=to, device_id_type=MESH)
            want += agent.astype(jnp.int32) * 8
            if not same:
                @pl.when(agent)
                def _():
                    to = at(0 * x, 0 * y + i // 2, z, 0)
                    pl.semaphore_signal(barrier, inc=1, device_id=to, device_id_type=MESH)
                want += source.astype(jnp.int32)
        pl.semaphore_wait(barrier, want)

    @pl.when(core == 0)
    def _():
        for n in range(9):
            i, j, ax, ay = blocks[n]
            source, agent, same = d_roles(n)
            if not same:
                @pl.when(source)
                def _():
                    to = at(0 * x + ax, 0 * y + ay, z, 0)
                    remote(d_input(n), d_place(n), a_send.at[0], a_recv, to).start()
        for n in range(9):
            i, j, ax, ay = blocks[n]
            source, agent, same = d_roles(n)
            @pl.when(agent)
            def _():
                if not same:
                    remote(d_place(n), d_place(n), a_send.at[0], a_recv, partner).wait_recv()
                for to in hubs:
                    remote(d_input(n) if same else d_place(n), d_place(n), a_send.at[1], d_recv.at[i - 1], to).start()

    def c_tree(src, q):
        dx, dy = x, lax.rem(y - src + NY, NY)
        if q % 2:
            dx, dy = lax.rem(NX - dx, NX), lax.rem(NY - dy, NY)
        if q >= 2:
            dx, dy = dy, dx
        along = (dy == 0) & (dx <= 2) | (dx == 3) & (dy >= 1)
        across = (dx >= 1) & (dy <= 2)
        hops = jnp.where((dx == 0) & (dy > 0), dy + 4, dx + dy)
        one, two = (q % 2, 2 + q % 2) if q < 2 else (2 + q % 2, q % 2)
        return [(one, along), (two, across)], hops

    def r_tree(c, way):
        hops = lax.rem((z - c if way == 0 else c - z) + NZ, NZ)
        return [(4 + way, hops <= 6)], hops

    def pass_on(live, src, dst, here, kids, sends, recv, to_core):
        def forward(ref):
            for n, (link, cond) in enumerate(kids):
                @pl.when(cond)
                def _():
                    remote(ref, dst, sends(n), recv, links[link]).start()
            to_core(ref)

        @pl.when(live & here)
        def _():
            forward(src)

        @pl.when(live & jnp.logical_not(here))
        def _():
            remote(dst, dst, sends(0), recv, partner).wait_recv()
            forward(dst)

    n_c = TILE // 4 // CCH * 6
    n_r = NB // CCH * 3

    pieces = [(0, 0), (1, 0), (2, 0), (1, 1), (2, 1), (3, 0), (3, 1), (2, 2), (3, 2), (3, 3)]

    def piece(k):
        i, j = pieces[k]
        return w.at[pl.ds(i * NB, NB), pl.ds(j * NB, NB)]

    def piece_value(i, j):
        return w[i * NB : (i + 1) * NB, j * NB : (j + 1) * NB]

    def hand_out(k):
        slot = 0
        for cond, kids in trees[1:]:
            @pl.when(cond)
            def _():
                for n, kid in enumerate(kids):
                    remote(piece(k), piece(k), p_send.at[slot + n], p_recv.at[k], kid).start()
            slot += len(kids)
        remote(piece(k), piece(k), p_send.at[slot], p_core.at[k], partner).start()

    @pl.when(core == 1)
    def _():
        @pl.loop(0, TURNS)
        def _(g):
            for q in range(4):
                for src_row in range(2):
                    kids, hops = c_tree(src_row, q)
                    i = g - LAG * hops
                    live = (i >= 0) & (i < n_c)
                    i = jnp.clip(i, 0, n_c - 1)
                    per = n_c // 6
                    b = i // per
                    rows = pl.ds(pl.multiple_of(q * (TILE // 4) + i % per * CCH, CCH), CCH)
                    src = cov.at[0, 0, b, 0, rows, :]
                    dst = pct.at[src_row, b, rows, :]
                    def to_core(ref):
                        for h in range(2):
                            @pl.when(i == n_c // 2 * (h + 1) - 1)
                            def _():
                                part = pl.ds(3 * h, 3), 0, pl.ds(q * (TILE // 4), TILE // 4)
                                home = pct.at[src_row, part[0], part[2], :]
                                @pl.when(hops == 0)
                                def _():
                                    remote(cov.at[0, 0, part[0], 0, part[2], :], home, k_send.at[0], c_core.at[src_row, q, h], partner).start()
                                @pl.when(hops != 0)
                                def _():
                                    remote(home, home, k_send.at[0], c_core.at[src_row, q, h], partner).start()
                    pass_on(live, src, dst, hops == 0, kids, lambda m: c_send.at[src_row, q, m], c_recv.at[src_row, q, i], to_core)
            for way in range(2):
                for c in range(2):
                    kids, hops = r_tree(c, way)
                    i = g - LAG * hops
                    live = (i >= 0) & (i < n_r)
                    i = jnp.clip(i, 0, n_r - 1)
                    per = n_r // 3
                    a = i // per
                    rows = pl.ds(pl.multiple_of(way * NB + i % per * CCH, CCH), CCH)
                    src = cov.at[a, 0, 0, 0, rows, :]
                    dst = rp.at[c, a, rows, :]
                    def to_core(ref):
                        if way == 0:
                            @pl.when(i % (n_r // 3) == n_r // 3 - 1)
                            def _():
                                home = rp.at[c, a, pl.ds(0, NB), :]
                                @pl.when(hops == 0)
                                def _():
                                    remote(cov.at[a, 0, 0, 0, pl.ds(0, NB), :], home, k_send.at[1], r_core.at[c, a], partner).start()
                                @pl.when(hops != 0)
                                def _():
                                    remote(home, home, k_send.at[1], r_core.at[c, a], partner).start()
                    pass_on(live, src, dst, hops == 0, kids, lambda m: r_send.at[c, way], r_recv.at[c, way, i], to_core)

        @pl.when((x == 0) & (y <= 1))
        def _():
            copy = pltpu.make_async_copy(cov.at[0, 0, :, 0], pct.at[y], local_sem)
            copy.start()
            copy.wait()
        @pl.when(z <= 1)
        def _():
            copy = pltpu.make_async_copy(cov.at[:, 0, 0, 0], rp.at[z], local_sem)
            copy.start()
            copy.wait()
        for copy in own:
            copy.start()
        for k in range(len(pieces)):
            remote(piece(k), piece(k), p_send.at[0], p_core.at[k], partner).wait_recv()

    @pl.when((core == 0) & jnp.logical_not(hub))
    def _():
        for copy in own:
            copy.start()
        for k in range(len(pieces)):
            remote(piece(k), piece(k), p_send.at[0], p_recv.at[k], partner).wait_recv()
            hand_out(k)

    @pl.when((core == 0) & hub)
    def _():
        first = s.at[pl.ds(0, NB), pl.ds(0, NB)]
        first_in = cov.at[0, 0, 0, 0, pl.ds(0, NB), pl.ds(0, NB)]

        @pl.when(z == 0)
        def _():
            for n, kid in enumerate(z_kids):
                remote(first_in, first, b_send.at[n], b_recv, kid).start()
            copy = pltpu.make_async_copy(first_in, first, local_sem)
            copy.start()
            copy.wait()
        @pl.when(z != 0)
        def _():
            remote(first, first, b_send.at[0], b_recv, partner).wait_recv()

        def block(i, j):
            return s[i * NB : (i + 1) * NB, j * NB : (j + 1) * NB]

        def wait_row(i):
            remote(d_rows[i], d_rows[i], b_send.at[0], d_recv.at[i - 1], partner).wait_recv()

        low = {}
        inv = {}

        def publish(i, j, value):
            w[i * NB : (i + 1) * NB, j * NB : (j + 1) * NB] = value
            hand_out(pieces.index((i, j)))

        def solve(i, j):
            rest = block(i, j)
            for n in range(j):
                rest = rest - dot_nt(low[i, n], low[j, n])
            low[i, j] = dot_nt(rest, inv[j])
            publish(i, j, low[i, j])

        for k in range(4):
            if k == 1:
                wait_row(1)
            if k > 0:
                solve(k, k - 1)
            piv = block(k, k)
            for j in range(k):
                piv = piv - dot_nt(low[k, j], low[k, j])
            if 0 < k < 3:
                wait_row(k + 1)
                for j in range(k):
                    solve(k + 1, j)
            inv[k] = jnp.concatenate(inverse_factor([piv[8 * i : 8 * i + 8] for i in range(16)]), axis=0)
            publish(k, k, inv[k])
            if k == 0:
                for copy in own:
                    copy.start()

    @pl.when(core == 0)
    def _():
        for q in range(4):
            for src_row in range(2):
                for h in range(2):
                    dst = pct.at[src_row, pl.ds(3 * h, 3), pl.ds(q * (TILE // 4), TILE // 4), :]
                    remote(dst, dst, b_send.at[0], c_core.at[src_row, q, h], partner).wait_recv()
        for c in range(2):
            for a in range(3):
                dst = rp.at[c, a, pl.ds(0, NB), :]
                remote(dst, dst, b_send.at[0], r_core.at[c, a], partner).wait_recv()

    inverse_rows = []
    for i in range(4):
        diag = piece_value(i, i)
        row_blocks = []
        for j in range(i):
            acc = None
            for n in range(j, i):
                part = dot_nn(piece_value(i, n), inverse_rows[n][:, j * NB : (j + 1) * NB])
                acc = part if acc is None else acc + part
            row_blocks.append(acc)
        if i == 0:
            inverse_rows.append(diag)
        else:
            left = -dot_nn(diag, jnp.concatenate(row_blocks, axis=1))
            inverse_rows.append(jnp.concatenate([left, diag], axis=1))
    tri = [split(v) for v in inverse_rows]
    nt, nn = ((1,), (1,)), ((1,), (0,))
    rows = [rp[c, :, pl.ds(core * HALF, HALF), :].reshape(3 * HALF, TILE) for c in range(2)]
    r_hi, r_lo = split(jnp.concatenate(rows, axis=1))
    c_parts = []
    for j in range(4):
        e = (j + 1) * NB
        got = dot3((r_hi[:, :e], r_lo[:, :e]), tri[j], nt)
        c_all[:, j * NB : e] = got
        c_parts.append(split(got))
    for j in range(4):
        cols = slice(j * NB, (j + 1) * NB)
        lhs = [jnp.concatenate([c_parts[i][h] for i in range(j, 4)], axis=1) for h in range(2)]
        rhs = [jnp.concatenate([tri[i][h][:, cols] for i in range(j, 4)], axis=0) for h in range(2)]
        hi, lo = split(dot3(lhs, rhs, nn))
        t_hi[:, cols] = hi
        t_lo[:, cols] = lo

    sub = lax.broadcasted_iota(jnp.int32, (3 * HALF, TILE), 0)
    lane = lax.broadcasted_iota(jnp.int32, (3 * HALF, TILE), 1)
    top = (sub < HALF) & (row < 2)

    def put(b):
        return pltpu.make_async_copy(mine.at[:, b], out.at[:, 0, b, 0], out_sem)

    pltpu.make_async_copy(mine, mine, in_sem).wait()

    @pl.loop(0, 6)
    def _(b):
        cols = jnp.concatenate([pct[0, b], pct[1, b]], axis=0)
        old = mine[:, b].reshape(3 * HALF, TILE)
        new = old - dot3((t_hi[...], t_lo[...]), split(cols), nn)
        mine[:, b] = jnp.where(top, 0.0, new).reshape(3, HALF, TILE)

        @pl.when((b == 0) & (z < 2))
        def _():
            panel = jnp.where(z == 0, c_all[:, :TILE], c_all[:, TILE:])
            above = top & (row * TILE + core * HALF + sub < z * TILE + lane)
            mine[:, 0] = jnp.where(above, 0.0, panel).reshape(3, HALF, TILE)
        put(b).start()

    def left_for(whole, send):
        remote(whole, whole, send, b_recv, partner).wait_send()

    @pl.when(core == 1)
    def _():
        for src_row in range(2):
            for q in range(4):
                kids, _ = c_tree(src_row, q)
                whole = pct.at[src_row, :, pl.ds(q * (TILE // 4), TILE // 4), :]
                for m, (_, cond) in enumerate(kids):
                    @pl.when(cond)
                    def _():
                        left_for(whole, c_send.at[src_row, q, m])
        for c in range(2):
            for way in range(2):
                kids, _ = r_tree(c, way)
                @pl.when(kids[0][1])
                def _():
                    left_for(rp.at[c, :, pl.ds(way * NB, NB), :], r_send.at[c, way])
        left_for(pct, k_send.at[0])
        left_for(rp.at[:, :, pl.ds(0, NB), :], k_send.at[1])

    @pl.when(core == 0)
    def _():
        @pl.when(trees[0][0])
        def _():
            for n in range(len(z_kids)):
                left_for(s.at[pl.ds(0, NB), pl.ds(0, NB)], b_send.at[n])
        for group, (sy, sz) in zip(outs, ((0, 0), (1, 0), (1, 1))):
            @pl.when((x == 0) & (y == sy) & (z == sz))
            def _():
                left_for(s.at[pl.ds(0, NB), pl.ds(0, len(group) * NB)], a_send.at[0])
        for n in range(9):
            @pl.when(d_roles(n)[1])
            def _():
                left_for(s.at[pl.ds(0, 2 * NB), :], a_send.at[1])
        all_pieces = pct.at[0, pl.ds(0, 5), pl.ds(0, NB), :]
        slot = 0
        for cond, kids in trees[1:]:
            @pl.when(cond)
            def _():
                for n in range(len(kids)):
                    left_for(all_pieces, p_send.at[slot + n])
            slot += len(kids)
        left_for(all_pieces, p_send.at[slot])

    pltpu.make_async_copy(mine, mine, out_sem).wait()


def on_device(covariance):
    dma = pltpu.SemaphoreType.DMA
    n_c = TILE // 4 // CCH * 6
    n_r = NB // CCH * 3
    return pl.pallas_call(
        panel_kernel,
        out_shape=jax.ShapeDtypeStruct((3, 1, 6, 1, HALF, TILE), F32),
        in_specs=[pl.BlockSpec(memory_space=pl.ANY)],
        out_specs=pl.BlockSpec(memory_space=pl.ANY),
        scratch_shapes=[
            pltpu.VMEM((2, 6, TILE, TILE), F32),
            pltpu.VMEM((2, 3, TILE, TILE), F32),
            pltpu.VMEM((PANEL, PANEL), F32),
            pltpu.VMEM((PANEL, PANEL), F32),
            pltpu.VMEM((3, 6, HALF, TILE), F32),
            pltpu.VMEM((3 * HALF, PANEL), F32),
            pltpu.VMEM((3 * HALF, PANEL), BF16),
            pltpu.VMEM((3 * HALF, PANEL), BF16),
            dma, dma((3,)), dma, dma((2, 4, n_c)), dma((2, 2, n_r)), dma((10,)), dma((2, 4, 2)), dma((2, 3)), dma((10,)),
            dma((7,)), dma((2,)), dma((2, 4, 2)), dma((2, 2)), dma((2,)), dma((7,)), dma, dma, dma,
        ],
        compiler_params=pltpu.CompilerParams(collective_id=0, has_side_effects=True),
        name="panel_step",
    )(covariance)


def solution(mesh):
    return jax.shard_map(
        on_device,
        mesh=mesh,
        in_specs=(P(None, "row", None, "col", None, None),),
        out_specs=P(None, "row", None, "col", "depth", None),
        check_vma=False,
    )
```

```python
import functools

import jax
import jax.numpy as jnp
from jax import lax
from jax.experimental import pallas as pl
from jax.experimental.pallas import tpu as pltpu
from jax.sharding import PartitionSpec as P

TILE = 256
PANEL = 512
NB = 128
NX = NY = 4
NZ = 8
CCH = 64
LAG = 2
TURNS = 6 * (TILE // 4 // CCH) + LAG * 7
HALF = TILE // 2
MESH = pl.DeviceIdType.MESH
HIGHEST = lax.Precision.HIGHEST
F32 = jnp.float32
BF16 = jnp.bfloat16


def dot_nt(a, b):
    dims = (((1,), (1,)), ((), ()))
    return lax.dot_general(a, b, dims, precision=HIGHEST, preferred_element_type=F32)


def dot_nn(a, b):
    dims = (((1,), (0,)), ((), ()))
    return lax.dot_general(a, b, dims, precision=HIGHEST, preferred_element_type=F32)


def split(x):
    hi = x.astype(BF16)
    return hi, (x - hi.astype(F32)).astype(BF16)


def dot3(a, b, dims):
    (ah, al), (bh, bl) = a, b
    dot = functools.partial(lax.dot_general, dimension_numbers=(dims, ((), ())), preferred_element_type=F32)
    return dot(ah, bh) + (dot(ah, bl) + dot(al, bh))


def lane_copy(v, k):
    return jnp.broadcast_to(v[:, k : k + 1], (8, NB))


def row_copy(v, k):
    return jnp.broadcast_to(v[k : k + 1, :], (8, NB))


def inverse_factor(rows):
    rows = list(rows)
    lane = lax.broadcasted_iota(jnp.int32, (8, NB), 1)
    sub = lax.broadcasted_iota(jnp.int32, (8, NB), 0)
    out = []
    for b in range(16):
        base = 8 * b
        cols = [[lane_copy(rows[i], base + k) for k in range(8)] for i in range(b, 16)]
        inside = (lane >= base) & (lane < base + 8)
        cur = jnp.where(inside, jnp.where(lane == sub + base, 1.0, 0.0), rows[b])
        diag = cols[0]
        scaled = jnp.zeros((8, NB), F32)
        for k in range(8):
            d = row_copy(diag[k], k)
            r = 1.0 / d
            scaled = jnp.where(sub == k, cur * lax.rsqrt(d), scaled)
            less = jnp.where(sub == k, diag[k] - 1.0, diag[k])
            for j in range(k + 1, 8):
                diag[j] = diag[j] - less * (row_copy(diag[k], j) * r)
            cur = cur - less * (row_copy(cur, k) * r)
        for i in range(b + 1, 16):
            acc = jnp.where(inside, 0.0, rows[i])
            for j in range(8):
                acc = acc - cols[i - b][j] * row_copy(cur, j)
            rows[i] = acc
        out.append(jnp.where(lane < base + 8, scaled, 0.0))
    return out


def panel_kernel(
    cov, out, pct, rp, s, w, mine, c_all, t_all, m3, t_hi, t_lo, p_hi, p_lo,
    b_recv, d_recv, a_recv, c_recv, r_recv, p_recv, c_core, r_core, p_core,
    b_send, a_send, c_send, r_send, k_send, p_send, in_sem, out_sem, local_sem,
):
    row = lax.axis_index("row")
    z = lax.axis_index("col")
    core = lax.axis_index("depth")
    x, y = row // NY, row % NY

    def at(xx, yy, zz, cc):
        return {"row": lax.rem(xx + NX, NX) * NY + lax.rem(yy + NY, NY), "col": lax.rem(zz + NZ, NZ), "depth": cc}

    def remote(src, dst, send, recv, to):
        return pltpu.make_async_remote_copy(src, dst, send, recv, device_id=to, device_id_type=MESH)

    partner = {"row": row, "col": z, "depth": 1 - core}
    links = [
        at(x + 1, y, z, 1), at(x - 1, y, z, 1), at(x, y + 1, z, 1),
        at(x, y - 1, z, 1), at(x, y, z + 1, 1), at(x, y, z - 1, 1),
    ]
    z_kids = [at(x, y, z + n, 0) for n in (4, 5, 3, 6, 2, 7, 1)]
    y_kids = [at(x, y + n, z, 0) for n in (2, 1, 3)]
    x_kids = [at(x + n, y, z, 0) for n in (2, 1, 3)]
    hub = row == 0
    trees = [(hub & (z == 0), z_kids), (hub, y_kids), (x == 0, x_kids)]

    own = [
        pltpu.make_async_copy(cov.at[:, 0, b, 0, pl.ds(core * HALF, HALF), :], mine.at[:, b], in_sem)
        for b in range(6)
    ]

    blocks = [
        (1, 0, 1, 0), (1, 1, 3, 0), (2, 0, 0, 1), (2, 1, 1, 1), (2, 2, 0, 1),
        (3, 0, 3, 1), (3, 1, 0, 2), (3, 2, 1, 1), (3, 3, 3, 1),
    ]

    def d_place(n):
        i, j, _, _ = blocks[n]
        return s.at[pl.ds(i * NB, NB), pl.ds(j * NB, NB)]

    def d_input(n):
        i, j, _, _ = blocks[n]
        return cov.at[0, 0, 0, 0, pl.ds(i % 2 * NB, NB), pl.ds(j % 2 * NB, NB)]

    def d_roles(n):
        i, j, ax, ay = blocks[n]
        source = (x == 0) & (y == i // 2) & (z == j // 2)
        agent = (x == ax) & (y == ay) & (z == j // 2)
        return source, agent, (ax, ay) == (0, i // 2)

    hubs = [at(0 * x, 0 * y, n + 0 * z, 0) for n in (4, 5, 3, 6, 2, 7, 1, 0)]
    outs = [[n for n in range(9) if blocks[n][0] // 2 == sy and blocks[n][1] // 2 == sz and not d_roles(n)[2]] for sy, sz in ((0, 0), (1, 0), (1, 1))]
    d_rows = {1: s.at[pl.ds(0, NB), pl.ds(0, 2 * NB)], 2: s.at[pl.ds(0, NB), pl.ds(0, 3 * NB)], 3: s.at[pl.ds(0, NB), :]}

    barrier = pltpu.get_barrier_semaphore()
    pl.semaphore_signal(barrier, inc=1, device_id=partner, device_id_type=MESH)

    @pl.when(core == 1)
    def _():
        for link in links:
            pl.semaphore_signal(barrier, inc=1, device_id=link, device_id_type=MESH)
        pl.semaphore_wait(barrier, 7)

    @pl.when(core == 0)
    def _():
        @pl.when(x != 0)
        def _():
            pl.semaphore_signal(barrier, inc=1, device_id=at(0 * x, y, z, 0), device_id_type=MESH)
        @pl.when((x == 0) & (y != 0))
        def _():
            pl.semaphore_signal(barrier, inc=1, device_id=at(x, 0 * y, z, 0), device_id_type=MESH)
        @pl.when(hub & (z != 0))
        def _():
            pl.semaphore_signal(barrier, inc=1, device_id=at(x, y, 0 * z, 0), device_id_type=MESH)
        want = 1 + sum(cond.astype(jnp.int32) * len(kids) for cond, kids in trees)
        for n in range(9):
            i, j, ax, ay = blocks[n]
            source, agent, same = d_roles(n)
            @pl.when(hub)
            def _():
                to = at(0 * x + ax, 0 * y + ay, 0 * z + j // 2, 0)
                pl.semaphore_signal(barrier, inc=1, device_id=to, device_id_type=MESH)
            want += agent.astype(jnp.int32) * 8
            if not same:
                @pl.when(agent)
                def _():
                    to = at(0 * x, 0 * y + i // 2, z, 0)
                    pl.semaphore_signal(barrier, inc=1, device_id=to, device_id_type=MESH)
                want += source.astype(jnp.int32)
        pl.semaphore_wait(barrier, want)

    @pl.when(core == 0)
    def _():
        for n in range(9):
            i, j, ax, ay = blocks[n]
            source, agent, same = d_roles(n)
            if not same:
                @pl.when(source)
                def _():
                    to = at(0 * x + ax, 0 * y + ay, z, 0)
                    remote(d_input(n), d_place(n), a_send.at[0], a_recv, to).start()
        for n in range(9):
            i, j, ax, ay = blocks[n]
            source, agent, same = d_roles(n)
            @pl.when(agent)
            def _():
                if not same:
                    remote(d_place(n), d_place(n), a_send.at[0], a_recv, partner).wait_recv()
                for to in hubs:
                    remote(d_input(n) if same else d_place(n), d_place(n), a_send.at[1], d_recv.at[i - 1], to).start()

    def c_tree(src, q):
        dx, dy = x, lax.rem(y - src + NY, NY)
        if q % 2:
            dx, dy = lax.rem(NX - dx, NX), lax.rem(NY - dy, NY)
        if q >= 2:
            dx, dy = dy, dx
        along = (dy == 0) & (dx <= 2) | (dx == 3) & (dy >= 1)
        across = (dx >= 1) & (dy <= 2)
        hops = jnp.where((dx == 0) & (dy > 0), dy + 4, dx + dy)
        one, two = (q % 2, 2 + q % 2) if q < 2 else (2 + q % 2, q % 2)
        return [(one, along), (two, across)], hops

    def r_tree(c, way):
        hops = lax.rem((z - c if way == 0 else c - z) + NZ, NZ)
        return [(4 + way, hops <= 6)], hops

    def pass_on(live, src, dst, here, kids, sends, recv, to_core):
        def forward(ref):
            for n, (link, cond) in enumerate(kids):
                @pl.when(cond)
                def _():
                    remote(ref, dst, sends(n), recv, links[link]).start()
            to_core(ref)

        @pl.when(live & here)
        def _():
            forward(src)

        @pl.when(live & jnp.logical_not(here))
        def _():
            remote(dst, dst, sends(0), recv, partner).wait_recv()
            forward(dst)

    n_c = TILE // 4 // CCH * 6
    n_r = NB // CCH * 3

    pieces = [(0, 0), (1, 0), (2, 0), (1, 1), (2, 1), (3, 0), (3, 1), (2, 2), (3, 2), (3, 3)]

    def piece(k):
        i, j = pieces[k]
        return w.at[pl.ds(i * NB, NB), pl.ds(j * NB, NB)]

    def piece_value(i, j):
        return w[i * NB : (i + 1) * NB, j * NB : (j + 1) * NB]

    def hand_out(k):
        slot = 0
        for cond, kids in trees[1:]:
            @pl.when(cond)
            def _():
                for n, kid in enumerate(kids):
                    remote(piece(k), piece(k), p_send.at[slot + n], p_recv.at[k], kid).start()
            slot += len(kids)
        remote(piece(k), piece(k), p_send.at[slot], p_core.at[k], partner).start()

    def take(k):
        @pl.when(core == 1)
        def _():
            remote(piece(k), piece(k), p_send.at[0], p_core.at[k], partner).wait_recv()

        @pl.when((core == 0) & jnp.logical_not(hub))
        def _():
            remote(piece(k), piece(k), p_send.at[0], p_recv.at[k], partner).wait_recv()
            hand_out(k)

    @pl.when(core == 1)
    def _():
        @pl.loop(0, TURNS)
        def _(g):
            for q in range(4):
                for src_row in range(2):
                    kids, hops = c_tree(src_row, q)
                    i = g - LAG * hops
                    live = (i >= 0) & (i < n_c)
                    i = jnp.clip(i, 0, n_c - 1)
                    per = n_c // 6
                    b = i // per
                    rows = pl.ds(pl.multiple_of(q * (TILE // 4) + i % per * CCH, CCH), CCH)
                    src = cov.at[0, 0, b, 0, rows, :]
                    dst = pct.at[src_row, b, rows, :]
                    def to_core(ref):
                        for h in range(2):
                            @pl.when(i == n_c // 2 * (h + 1) - 1)
                            def _():
                                part = pl.ds(3 * h, 3), 0, pl.ds(q * (TILE // 4), TILE // 4)
                                home = pct.at[src_row, part[0], part[2], :]
                                @pl.when(hops == 0)
                                def _():
                                    remote(cov.at[0, 0, part[0], 0, part[2], :], home, k_send.at[0], c_core.at[src_row, q, h], partner).start()
                                @pl.when(hops != 0)
                                def _():
                                    remote(home, home, k_send.at[0], c_core.at[src_row, q, h], partner).start()
                    pass_on(live, src, dst, hops == 0, kids, lambda m: c_send.at[src_row, q, m], c_recv.at[src_row, q, i], to_core)
            for way in range(2):
                for c in range(2):
                    kids, hops = r_tree(c, way)
                    i = g - LAG * hops
                    live = (i >= 0) & (i < n_r)
                    i = jnp.clip(i, 0, n_r - 1)
                    per = n_r // 3
                    a = i // per
                    rows = pl.ds(pl.multiple_of(way * NB + i % per * CCH, CCH), CCH)
                    src = cov.at[a, 0, 0, 0, rows, :]
                    dst = rp.at[c, a, rows, :]
                    def to_core(ref):
                        if way == 0:
                            @pl.when(i % (n_r // 3) == n_r // 3 - 1)
                            def _():
                                home = rp.at[c, a, pl.ds(0, NB), :]
                                @pl.when(hops == 0)
                                def _():
                                    remote(cov.at[a, 0, 0, 0, pl.ds(0, NB), :], home, k_send.at[1], r_core.at[c, a], partner).start()
                                @pl.when(hops != 0)
                                def _():
                                    remote(home, home, k_send.at[1], r_core.at[c, a], partner).start()
                    pass_on(live, src, dst, hops == 0, kids, lambda m: r_send.at[c, way], r_recv.at[c, way, i], to_core)

        @pl.when((x == 0) & (y <= 1))
        def _():
            copy = pltpu.make_async_copy(cov.at[0, 0, :, 0], pct.at[y], local_sem)
            copy.start()
            copy.wait()
        @pl.when(z <= 1)
        def _():
            copy = pltpu.make_async_copy(cov.at[:, 0, 0, 0], rp.at[z], local_sem)
            copy.start()
            copy.wait()
        for copy in own:
            copy.start()

    @pl.when((core == 0) & jnp.logical_not(hub))
    def _():
        for copy in own:
            copy.start()

    @pl.when((core == 0) & hub)
    def _():
        first = s.at[pl.ds(0, NB), pl.ds(0, NB)]
        first_in = cov.at[0, 0, 0, 0, pl.ds(0, NB), pl.ds(0, NB)]

        @pl.when(z == 0)
        def _():
            for n, kid in enumerate(z_kids):
                remote(first_in, first, b_send.at[n], b_recv, kid).start()
            copy = pltpu.make_async_copy(first_in, first, local_sem)
            copy.start()
            copy.wait()
        @pl.when(z != 0)
        def _():
            remote(first, first, b_send.at[0], b_recv, partner).wait_recv()

        def block(i, j):
            return s[i * NB : (i + 1) * NB, j * NB : (j + 1) * NB]

        def wait_row(i):
            remote(d_rows[i], d_rows[i], b_send.at[0], d_recv.at[i - 1], partner).wait_recv()

        low = {}
        inv = {}

        def publish(i, j, value):
            w[i * NB : (i + 1) * NB, j * NB : (j + 1) * NB] = value
            hand_out(pieces.index((i, j)))

        def product(a, b):
            return dot3(a, b, ((1,), (1,)))

        def solve(i, j):
            rest = block(i, j)
            for n in range(j):
                rest = rest - product(low[i, n], low[j, n])
            got = product(split(rest), inv[j])
            low[i, j] = split(got)
            publish(i, j, got)

        for k in range(4):
            if k == 1:
                wait_row(1)
            if k > 0:
                solve(k, k - 1)
            piv = block(k, k)
            for j in range(k):
                piv = piv - product(low[k, j], low[k, j])
            if 0 < k < 3:
                wait_row(k + 1)
                for j in range(k):
                    solve(k + 1, j)
            wk = jnp.concatenate(inverse_factor([piv[8 * i : 8 * i + 8] for i in range(16)]), axis=0)
            publish(k, k, wk)
            inv[k] = split(wk)
            if k == 0:
                for copy in own:
                    copy.start()

    late = len(pieces) - 2
    last = len(pieces) - 1
    for k in range(late):
        take(k)
    nt, nn = ((1,), (1,)), ((1,), (0,))

    inverse_rows = []
    for i in range(4):
        if i == 3:
            take(late)
        row_blocks = []
        for j in range(i):
            acc = None
            for n in range(j, i):
                part = dot_nn(piece_value(i, n), inverse_rows[n][:, j * NB : (j + 1) * NB])
                acc = part if acc is None else acc + part
            row_blocks.append(acc)
        if i == 0:
            inverse_rows.append(piece_value(0, 0))
        elif i < 3:
            left = -dot_nn(piece_value(i, i), jnp.concatenate(row_blocks, axis=1))
            inverse_rows.append(jnp.concatenate([left, piece_value(i, i)], axis=1))
        else:
            m3[...] = jnp.concatenate(row_blocks, axis=1)
    tri = [split(v) for v in inverse_rows]

    passes_on = (core == 0) & (x == 0)

    @pl.when(passes_on)
    def _():
        take(last)

    @pl.when(core == 0)
    def _():
        for q in range(4):
            for src_row in range(2):
                for h in range(2):
                    dst = pct.at[src_row, pl.ds(3 * h, 3), pl.ds(q * (TILE // 4), TILE // 4), :]
                    remote(dst, dst, b_send.at[0], c_core.at[src_row, q, h], partner).wait_recv()
        for c in range(2):
            for a in range(3):
                dst = rp.at[c, a, pl.ds(0, NB), :]
                remote(dst, dst, b_send.at[0], r_core.at[c, a], partner).wait_recv()

    rows = [rp[c, :, pl.ds(core * HALF, HALF), :].reshape(3 * HALF, TILE) for c in range(2)]
    r_hi, r_lo = split(jnp.concatenate(rows, axis=1))
    c_parts = []
    for j in range(3):
        e = (j + 1) * NB
        got = dot3((r_hi[:, :e], r_lo[:, :e]), tri[j], nt)
        c_all[:, j * NB : e] = got
        c_parts.append(split(got))
    for j in range(3):
        cols = slice(j * NB, (j + 1) * NB)
        lhs = [jnp.concatenate([c_parts[i][h] for i in range(j, 3)], axis=1) for h in range(2)]
        rhs = [jnp.concatenate([tri[i][h][:, cols] for i in range(j, 3)], axis=0) for h in range(2)]
        t_all[:, cols] = dot3(lhs, rhs, nn)

    @pl.loop(0, 6)
    def _(b):
        for c in range(2):
            hi, lo = split(pct[c, b])
            p_hi[b, c * TILE : (c + 1) * TILE] = hi
            p_lo[b, c * TILE : (c + 1) * TILE] = lo

    @pl.when(jnp.logical_not(passes_on))
    def _():
        take(last)

    left = -dot_nn(piece_value(3, 3), m3[...])
    end = split(jnp.concatenate([left, piece_value(3, 3)], axis=1))
    c_last = dot3((r_hi, r_lo), end, nt)
    c_all[:, 3 * NB :] = c_last
    t_last = dot3(split(c_last), end, nn)
    hi, lo = split(t_all[...] + t_last[:, : 3 * NB])
    t_hi[:, : 3 * NB] = hi
    t_lo[:, : 3 * NB] = lo
    hi, lo = split(t_last[:, 3 * NB :])
    t_hi[:, 3 * NB :] = hi
    t_lo[:, 3 * NB :] = lo

    sub = lax.broadcasted_iota(jnp.int32, (3 * HALF, TILE), 0)
    lane = lax.broadcasted_iota(jnp.int32, (3 * HALF, TILE), 1)
    top = (sub < HALF) & (row < 2)

    def put(b):
        return pltpu.make_async_copy(mine.at[:, b], out.at[:, 0, b, 0], out_sem)

    pltpu.make_async_copy(mine, mine, in_sem).wait()

    @pl.loop(0, 6)
    def _(b):
        old = mine[:, b].reshape(3 * HALF, TILE)
        new = old - dot3((t_hi[...], t_lo[...]), (p_hi[b], p_lo[b]), nn)
        mine[:, b] = jnp.where(top, 0.0, new).reshape(3, HALF, TILE)

        @pl.when((b == 0) & (z < 2))
        def _():
            panel = jnp.where(z == 0, c_all[:, :TILE], c_all[:, TILE:])
            above = top & (row * TILE + core * HALF + sub < z * TILE + lane)
            mine[:, 0] = jnp.where(above, 0.0, panel).reshape(3, HALF, TILE)
        put(b).start()

    def left_for(whole, send):
        remote(whole, whole, send, b_recv, partner).wait_send()

    @pl.when(core == 1)
    def _():
        for src_row in range(2):
            for q in range(4):
                kids, _ = c_tree(src_row, q)
                whole = pct.at[src_row, :, pl.ds(q * (TILE // 4), TILE // 4), :]
                for m, (_, cond) in enumerate(kids):
                    @pl.when(cond)
                    def _():
                        left_for(whole, c_send.at[src_row, q, m])
        for c in range(2):
            for way in range(2):
                kids, _ = r_tree(c, way)
                @pl.when(kids[0][1])
                def _():
                    left_for(rp.at[c, :, pl.ds(way * NB, NB), :], r_send.at[c, way])
        left_for(pct, k_send.at[0])
        left_for(rp.at[:, :, pl.ds(0, NB), :], k_send.at[1])

    @pl.when(core == 0)
    def _():
        @pl.when(trees[0][0])
        def _():
            for n in range(len(z_kids)):
                left_for(s.at[pl.ds(0, NB), pl.ds(0, NB)], b_send.at[n])
        for group, (sy, sz) in zip(outs, ((0, 0), (1, 0), (1, 1))):
            @pl.when((x == 0) & (y == sy) & (z == sz))
            def _():
                left_for(s.at[pl.ds(0, NB), pl.ds(0, len(group) * NB)], a_send.at[0])
        for n in range(9):
            @pl.when(d_roles(n)[1])
            def _():
                left_for(s.at[pl.ds(0, 2 * NB), :], a_send.at[1])
        all_pieces = pct.at[0, pl.ds(0, 5), pl.ds(0, NB), :]
        slot = 0
        for cond, kids in trees[1:]:
            @pl.when(cond)
            def _():
                for n in range(len(kids)):
                    left_for(all_pieces, p_send.at[slot + n])
            slot += len(kids)
        left_for(all_pieces, p_send.at[slot])

    pltpu.make_async_copy(mine, mine, out_sem).wait()


def on_device(covariance):
    dma = pltpu.SemaphoreType.DMA
    n_c = TILE // 4 // CCH * 6
    n_r = NB // CCH * 3
    return pl.pallas_call(
        panel_kernel,
        out_shape=jax.ShapeDtypeStruct((3, 1, 6, 1, HALF, TILE), F32),
        in_specs=[pl.BlockSpec(memory_space=pltpu.HBM)],
        out_specs=pl.BlockSpec(memory_space=pl.ANY),
        scratch_shapes=[
            pltpu.VMEM((2, 6, TILE, TILE), F32),
            pltpu.VMEM((2, 3, TILE, TILE), F32),
            pltpu.VMEM((PANEL, PANEL), F32),
            pltpu.VMEM((PANEL, PANEL), F32),
            pltpu.VMEM((3, 6, HALF, TILE), F32),
            pltpu.VMEM((3 * HALF, PANEL), F32),
            pltpu.VMEM((3 * HALF, 3 * NB), F32),
            pltpu.VMEM((NB, 3 * NB), F32),
            pltpu.VMEM((3 * HALF, PANEL), BF16),
            pltpu.VMEM((3 * HALF, PANEL), BF16),
            pltpu.VMEM((6, PANEL, TILE), BF16),
            pltpu.VMEM((6, PANEL, TILE), BF16),
            dma, dma((3,)), dma, dma((2, 4, n_c)), dma((2, 2, n_r)), dma((10,)), dma((2, 4, 2)), dma((2, 3)), dma((10,)),
            dma((7,)), dma((2,)), dma((2, 4, 2)), dma((2, 2)), dma((2,)), dma((7,)), dma, dma, dma,
        ],
        compiler_params=pltpu.CompilerParams(collective_id=0, has_side_effects=True, vmem_limit_bytes=48 * 1024 * 1024),
        name="panel_step",
    )(covariance)


def solution(mesh):
    return jax.shard_map(
        on_device,
        mesh=mesh,
        in_specs=(P(None, "row", None, "col", None, None),),
        out_specs=P(None, "row", None, "col", "depth", None),
        check_vma=False,
    )
```

```python
import functools

import jax
import jax.numpy as jnp
from jax import lax
from jax.experimental import pallas as pl
from jax.experimental.pallas import tpu as pltpu
from jax.sharding import PartitionSpec as P

TILE = 256
PANEL = 512
NB = 128
NX = NY = 4
NZ = 8
CCH = 64
LAG = 3
TURNS = 6 * (TILE // 4 // CCH) + LAG * 7
HALF = TILE // 2
MESH = pl.DeviceIdType.MESH
HIGHEST = lax.Precision.HIGHEST
F32 = jnp.float32
BF16 = jnp.bfloat16


def dot_nt(a, b):
    dims = (((1,), (1,)), ((), ()))
    return lax.dot_general(a, b, dims, precision=HIGHEST, preferred_element_type=F32)


def dot_nn(a, b):
    dims = (((1,), (0,)), ((), ()))
    return lax.dot_general(a, b, dims, precision=HIGHEST, preferred_element_type=F32)


def split(x):
    hi = x.astype(BF16)
    return hi, (x - hi.astype(F32)).astype(BF16)


def dot3(a, b, dims):
    (ah, al), (bh, bl) = a, b
    dot = functools.partial(lax.dot_general, dimension_numbers=(dims, ((), ())), preferred_element_type=F32)
    return dot(ah, bh) + (dot(ah, bl) + dot(al, bh))


def lane_copy(v, k):
    return jnp.broadcast_to(v[:, k : k + 1], (8, NB))


def row_copy(v, k):
    return jnp.broadcast_to(v[k : k + 1, :], (8, NB))


def inverse_factor(rows):
    rows = list(rows)
    lane = lax.broadcasted_iota(jnp.int32, (8, NB), 1)
    sub = lax.broadcasted_iota(jnp.int32, (8, NB), 0)
    out = []
    for b in range(16):
        base = 8 * b
        cols = [[lane_copy(rows[i], base + k) for k in range(8)] for i in range(b, 16)]
        inside = (lane >= base) & (lane < base + 8)
        cur = jnp.where(inside, jnp.where(lane == sub + base, 1.0, 0.0), rows[b])
        diag = cols[0]
        scaled = jnp.zeros((8, NB), F32)
        for k in range(8):
            d = row_copy(diag[k], k)
            r = 1.0 / d
            scaled = jnp.where(sub == k, cur * lax.rsqrt(d), scaled)
            less = jnp.where(sub == k, diag[k] - 1.0, diag[k])
            for j in range(k + 1, 8):
                diag[j] = diag[j] - less * (row_copy(diag[k], j) * r)
            cur = cur - less * (row_copy(cur, k) * r)
        for i in range(b + 1, 16):
            acc = jnp.where(inside, 0.0, rows[i])
            for j in range(8):
                acc = acc - cols[i - b][j] * row_copy(cur, j)
            rows[i] = acc
        out.append(jnp.where(lane < base + 8, scaled, 0.0))
    return out


def panel_kernel(
    cov, out, pct, rp, s, w, mine, c_all, t_all, m3, t_hi, t_lo, p_hi, p_lo,
    b_recv, d_recv, a_recv, c_recv, r_recv, p_recv, c_core, r_core, p_core,
    b_send, a_send, c_send, r_send, k_send, p_send, in_sem, out_sem, local_sem, rows_sem, cols_sem,
):
    row = lax.axis_index("row")
    z = lax.axis_index("col")
    core = lax.axis_index("depth")
    x, y = row // NY, row % NY

    def at(xx, yy, zz, cc):
        return {"row": lax.rem(xx + NX, NX) * NY + lax.rem(yy + NY, NY), "col": lax.rem(zz + NZ, NZ), "depth": cc}

    def remote(src, dst, send, recv, to):
        return pltpu.make_async_remote_copy(src, dst, send, recv, device_id=to, device_id_type=MESH)

    partner = {"row": row, "col": z, "depth": 1 - core}
    links = [
        at(x + 1, y, z, 1), at(x - 1, y, z, 1), at(x, y + 1, z, 1),
        at(x, y - 1, z, 1), at(x, y, z + 1, 1), at(x, y, z - 1, 1),
    ]
    z_kids = [at(x, y, z + n, 0) for n in (4, 5, 3, 6, 2, 7, 1)]
    y_kids = [at(x, y + n, z, 0) for n in (2, 1, 3)]
    x_kids = [at(x + n, y, z, 0) for n in (2, 1, 3)]
    hub = row == 0
    trees = [(hub & (z == 0), z_kids), (hub, y_kids), (x == 0, x_kids)]

    own = [
        pltpu.make_async_copy(cov.at[:, 0, b, 0, pl.ds(core * HALF, HALF), :], mine.at[:, b], in_sem)
        for b in range(6)
    ]

    blocks = [
        (1, 0, 1, 0), (1, 1, 3, 0), (2, 0, 0, 1), (2, 1, 1, 1), (2, 2, 0, 1),
        (3, 0, 3, 1), (3, 1, 0, 2), (3, 2, 1, 1), (3, 3, 3, 1),
    ]

    def d_place(n):
        i, j, _, _ = blocks[n]
        return s.at[pl.ds(i * NB, NB), pl.ds(j * NB, NB)]

    def d_input(n):
        i, j, _, _ = blocks[n]
        return cov.at[0, 0, 0, 0, pl.ds(i % 2 * NB, NB), pl.ds(j % 2 * NB, NB)]

    def d_roles(n):
        i, j, ax, ay = blocks[n]
        source = (x == 0) & (y == i // 2) & (z == j // 2)
        agent = (x == ax) & (y == ay) & (z == j // 2)
        return source, agent, (ax, ay) == (0, i // 2)

    hubs = [at(0 * x, 0 * y, n + 0 * z, 0) for n in (4, 5, 3, 6, 2, 7, 1, 0)]
    outs = [[n for n in range(9) if blocks[n][0] // 2 == sy and blocks[n][1] // 2 == sz and not d_roles(n)[2]] for sy, sz in ((0, 0), (1, 0), (1, 1))]
    d_rows = {1: s.at[pl.ds(0, NB), pl.ds(0, 2 * NB)], 2: s.at[pl.ds(0, NB), pl.ds(0, 3 * NB)], 3: s.at[pl.ds(0, NB), :]}

    barrier = pltpu.get_barrier_semaphore()
    pl.semaphore_signal(barrier, inc=1, device_id=partner, device_id_type=MESH)

    @pl.when(core == 1)
    def _():
        for link in links:
            pl.semaphore_signal(barrier, inc=1, device_id=link, device_id_type=MESH)
        pl.semaphore_wait(barrier, 7)

    @pl.when(core == 0)
    def _():
        @pl.when(x != 0)
        def _():
            pl.semaphore_signal(barrier, inc=1, device_id=at(0 * x, y, z, 0), device_id_type=MESH)
        @pl.when((x == 0) & (y != 0))
        def _():
            pl.semaphore_signal(barrier, inc=1, device_id=at(x, 0 * y, z, 0), device_id_type=MESH)
        @pl.when(hub & (z != 0))
        def _():
            pl.semaphore_signal(barrier, inc=1, device_id=at(x, y, 0 * z, 0), device_id_type=MESH)
        want = 1 + sum(cond.astype(jnp.int32) * len(kids) for cond, kids in trees)
        for n in range(9):
            i, j, ax, ay = blocks[n]
            source, agent, same = d_roles(n)
            @pl.when(hub)
            def _():
                to = at(0 * x + ax, 0 * y + ay, 0 * z + j // 2, 0)
                pl.semaphore_signal(barrier, inc=1, device_id=to, device_id_type=MESH)
            want += agent.astype(jnp.int32) * 8
            if not same:
                @pl.when(agent)
                def _():
                    to = at(0 * x, 0 * y + i // 2, z, 0)
                    pl.semaphore_signal(barrier, inc=1, device_id=to, device_id_type=MESH)
                want += source.astype(jnp.int32)
        pl.semaphore_wait(barrier, want)

    @pl.when(core == 0)
    def _():
        for n in range(9):
            i, j, ax, ay = blocks[n]
            source, agent, same = d_roles(n)
            if not same:
                @pl.when(source)
                def _():
                    to = at(0 * x + ax, 0 * y + ay, z, 0)
                    remote(d_input(n), d_place(n), a_send.at[0], a_recv, to).start()
        for n in range(9):
            i, j, ax, ay = blocks[n]
            source, agent, same = d_roles(n)
            @pl.when(agent)
            def _():
                if not same:
                    remote(d_place(n), d_place(n), a_send.at[0], a_recv, partner).wait_recv()
                for to in hubs:
                    remote(d_input(n) if same else d_place(n), d_place(n), a_send.at[1], d_recv.at[i - 1], to).start()

    def c_tree(src, q):
        dx, dy = x, lax.rem(y - src + NY, NY)
        if q % 2:
            dx, dy = lax.rem(NX - dx, NX), lax.rem(NY - dy, NY)
        if q >= 2:
            dx, dy = dy, dx
        along = (dy == 0) & (dx <= 2) | (dx == 3) & (dy >= 1)
        across = (dx >= 1) & (dy <= 2)
        hops = jnp.where((dx == 0) & (dy > 0), dy + 4, dx + dy)
        one, two = (q % 2, 2 + q % 2) if q < 2 else (2 + q % 2, q % 2)
        return [(one, along), (two, across)], hops

    def r_tree(c, way):
        hops = lax.rem((z - c if way == 0 else c - z) + NZ, NZ)
        return [(4 + way, hops <= 6)], hops

    def pass_on(live, src, dst, here, kids, sends, recv, to_core):
        def forward(ref):
            for n, (link, cond) in enumerate(kids):
                @pl.when(cond)
                def _():
                    remote(ref, dst, sends(n), recv, links[link]).start()
            to_core(ref)

        @pl.when(live & here)
        def _():
            forward(src)

        @pl.when(live & jnp.logical_not(here))
        def _():
            remote(dst, dst, sends(0), recv, partner).wait_recv()
            forward(dst)

    n_c = TILE // 4 // CCH * 6
    n_r = NB // CCH * 3

    pieces = [(0, 0), (1, 0), (2, 0), (1, 1), (2, 1), (3, 0), (3, 1), (2, 2), (3, 2), (3, 3)]

    def piece(k):
        i, j = pieces[k]
        return w.at[pl.ds(i * NB, NB), pl.ds(j * NB, NB)]

    def piece_value(i, j):
        return w[i * NB : (i + 1) * NB, j * NB : (j + 1) * NB]

    def hand_out(k):
        slot = 0
        for cond, kids in trees[1:]:
            @pl.when(cond)
            def _():
                for n, kid in enumerate(kids):
                    remote(piece(k), piece(k), p_send.at[slot + n], p_recv.at[k], kid).start()
            slot += len(kids)
        remote(piece(k), piece(k), p_send.at[slot], p_core.at[k], partner).start()

    def take(k):
        @pl.when(core == 1)
        def _():
            remote(piece(k), piece(k), p_send.at[0], p_core.at[k], partner).wait_recv()

        @pl.when((core == 0) & jnp.logical_not(hub))
        def _():
            remote(piece(k), piece(k), p_send.at[0], p_recv.at[k], partner).wait_recv()
            hand_out(k)

    own_rows = (x == 0) & (y <= 1) & (core == 1)
    own_cols = (z <= 1) & (core == 1)

    @pl.when(own_rows)
    def _():
        for b in range(6):
            pltpu.make_async_copy(cov.at[0, 0, b, 0], pct.at[y, b], rows_sem).start()

    @pl.when(own_cols)
    def _():
        for a in range(3):
            pltpu.make_async_copy(cov.at[a, 0, 0, 0], rp.at[z, a], cols_sem).start()

    @pl.when(core == 1)
    def _():
        @pl.loop(0, TURNS)
        def _(g):
            for q in range(4):
                for src_row in range(2):
                    kids, hops = c_tree(src_row, q)
                    i = g - LAG * hops
                    live = (i >= 0) & (i < n_c)
                    i = jnp.clip(i, 0, n_c - 1)
                    per = n_c // 6
                    b = i // per
                    rows = pl.ds(pl.multiple_of(q * (TILE // 4) + i % per * CCH, CCH), CCH)
                    src = cov.at[0, 0, b, 0, rows, :]
                    dst = pct.at[src_row, b, rows, :]
                    def to_core(ref):
                        for h in range(2):
                            @pl.when(i == n_c // 2 * (h + 1) - 1)
                            def _():
                                part = pl.ds(3 * h, 3), 0, pl.ds(q * (TILE // 4), TILE // 4)
                                home = pct.at[src_row, part[0], part[2], :]
                                @pl.when(hops == 0)
                                def _():
                                    remote(cov.at[0, 0, part[0], 0, part[2], :], home, k_send.at[0], c_core.at[src_row, q, h], partner).start()
                                @pl.when(hops != 0)
                                def _():
                                    remote(home, home, k_send.at[0], c_core.at[src_row, q, h], partner).start()
                    pass_on(live, src, dst, hops == 0, kids, lambda m: c_send.at[src_row, q, m], c_recv.at[src_row, q, i], to_core)
            for way in range(2):
                for c in range(2):
                    kids, hops = r_tree(c, way)
                    i = g - LAG * hops
                    live = (i >= 0) & (i < n_r)
                    i = jnp.clip(i, 0, n_r - 1)
                    per = n_r // 3
                    a = i // per
                    rows = pl.ds(pl.multiple_of(way * NB + i % per * CCH, CCH), CCH)
                    src = cov.at[a, 0, 0, 0, rows, :]
                    dst = rp.at[c, a, rows, :]
                    def to_core(ref):
                        if way == 0:
                            @pl.when(i % (n_r // 3) == n_r // 3 - 1)
                            def _():
                                home = rp.at[c, a, pl.ds(0, NB), :]
                                @pl.when(hops == 0)
                                def _():
                                    remote(cov.at[a, 0, 0, 0, pl.ds(0, NB), :], home, k_send.at[1], r_core.at[c, a], partner).start()
                                @pl.when(hops != 0)
                                def _():
                                    remote(home, home, k_send.at[1], r_core.at[c, a], partner).start()
                    pass_on(live, src, dst, hops == 0, kids, lambda m: r_send.at[c, way], r_recv.at[c, way, i], to_core)

        for copy in own:
            copy.start()

    @pl.when((core == 0) & jnp.logical_not(hub))
    def _():
        for copy in own:
            copy.start()

    @pl.when((core == 0) & hub)
    def _():
        first = s.at[pl.ds(0, NB), pl.ds(0, NB)]
        first_in = cov.at[0, 0, 0, 0, pl.ds(0, NB), pl.ds(0, NB)]

        @pl.when(z == 0)
        def _():
            for n, kid in enumerate(z_kids):
                remote(first_in, first, b_send.at[n], b_recv, kid).start()
            copy = pltpu.make_async_copy(first_in, first, local_sem)
            copy.start()
            copy.wait()
        @pl.when(z != 0)
        def _():
            remote(first, first, b_send.at[0], b_recv, partner).wait_recv()

        def block(i, j):
            return s[i * NB : (i + 1) * NB, j * NB : (j + 1) * NB]

        def wait_row(i):
            remote(d_rows[i], d_rows[i], b_send.at[0], d_recv.at[i - 1], partner).wait_recv()

        low = {}
        inv = {}

        def publish(i, j, value):
            w[i * NB : (i + 1) * NB, j * NB : (j + 1) * NB] = value
            hand_out(pieces.index((i, j)))

        def product(a, b):
            return dot3(a, b, ((1,), (1,)))

        def solve(i, j):
            rest = block(i, j)
            for n in range(j):
                rest = rest - product(low[i, n], low[j, n])
            got = product(split(rest), inv[j])
            low[i, j] = split(got)
            publish(i, j, got)

        for k in range(4):
            if k == 1:
                wait_row(1)
            if k > 0:
                solve(k, k - 1)
            piv = block(k, k)
            for j in range(k):
                piv = piv - product(low[k, j], low[k, j])
            if 0 < k < 3:
                wait_row(k + 1)
                for j in range(k):
                    solve(k + 1, j)
            wk = jnp.concatenate(inverse_factor([piv[8 * i : 8 * i + 8] for i in range(16)]), axis=0)
            publish(k, k, wk)
            inv[k] = split(wk)
            if k == 0:
                for copy in own:
                    copy.start()

    late = len(pieces) - 2
    last = len(pieces) - 1
    for k in range(late):
        take(k)
    nt, nn = ((1,), (1,)), ((1,), (0,))

    inverse_rows = []
    for i in range(4):
        if i == 3:
            take(late)
        row_blocks = []
        for j in range(i):
            acc = None
            for n in range(j, i):
                part = dot_nn(piece_value(i, n), inverse_rows[n][:, j * NB : (j + 1) * NB])
                acc = part if acc is None else acc + part
            row_blocks.append(acc)
        if i == 0:
            inverse_rows.append(piece_value(0, 0))
        elif i < 3:
            left = -dot_nn(piece_value(i, i), jnp.concatenate(row_blocks, axis=1))
            inverse_rows.append(jnp.concatenate([left, piece_value(i, i)], axis=1))
        else:
            m3[...] = jnp.concatenate(row_blocks, axis=1)
    tri = [split(v) for v in inverse_rows]

    passes_on = (core == 0) & (x == 0)

    @pl.when(passes_on)
    def _():
        take(last)

    @pl.when(core == 0)
    def _():
        for q in range(4):
            for src_row in range(2):
                for h in range(2):
                    dst = pct.at[src_row, pl.ds(3 * h, 3), pl.ds(q * (TILE // 4), TILE // 4), :]
                    remote(dst, dst, b_send.at[0], c_core.at[src_row, q, h], partner).wait_recv()
        for c in range(2):
            for a in range(3):
                dst = rp.at[c, a, pl.ds(0, NB), :]
                remote(dst, dst, b_send.at[0], r_core.at[c, a], partner).wait_recv()

    @pl.when(own_rows)
    def _():
        pltpu.make_async_copy(pct.at[y], pct.at[y], rows_sem).wait()

    @pl.when(own_cols)
    def _():
        pltpu.make_async_copy(rp.at[z], rp.at[z], cols_sem).wait()

    rows = [rp[c, :, pl.ds(core * HALF, HALF), :].reshape(3 * HALF, TILE) for c in range(2)]
    r_hi, r_lo = split(jnp.concatenate(rows, axis=1))
    c_parts = []
    for j in range(3):
        e = (j + 1) * NB
        got = dot3((r_hi[:, :e], r_lo[:, :e]), tri[j], nt)
        c_all[:, j * NB : e] = got
        c_parts.append(split(got))
    for j in range(3):
        cols = slice(j * NB, (j + 1) * NB)
        lhs = [jnp.concatenate([c_parts[i][h] for i in range(j, 3)], axis=1) for h in range(2)]
        rhs = [jnp.concatenate([tri[i][h][:, cols] for i in range(j, 3)], axis=0) for h in range(2)]
        t_all[:, cols] = dot3(lhs, rhs, nn)

    @pl.loop(0, 6)
    def _(b):
        for c in range(2):
            hi, lo = split(pct[c, b])
            p_hi[b, c * TILE : (c + 1) * TILE] = hi
            p_lo[b, c * TILE : (c + 1) * TILE] = lo

    @pl.when(jnp.logical_not(passes_on))
    def _():
        take(last)

    left = -dot_nn(piece_value(3, 3), m3[...])
    end = split(jnp.concatenate([left, piece_value(3, 3)], axis=1))
    c_last = dot3((r_hi, r_lo), end, nt)
    c_all[:, 3 * NB :] = c_last
    t_last = dot3(split(c_last), end, nn)
    hi, lo = split(t_all[...] + t_last[:, : 3 * NB])
    t_hi[:, : 3 * NB] = hi
    t_lo[:, : 3 * NB] = lo
    hi, lo = split(t_last[:, 3 * NB :])
    t_hi[:, 3 * NB :] = hi
    t_lo[:, 3 * NB :] = lo

    sub = lax.broadcasted_iota(jnp.int32, (3 * HALF, TILE), 0)
    lane = lax.broadcasted_iota(jnp.int32, (3 * HALF, TILE), 1)
    top = (sub < HALF) & (row < 2)

    def put(b):
        return pltpu.make_async_copy(mine.at[:, b], out.at[:, 0, b, 0], out_sem)

    pltpu.make_async_copy(mine, mine, in_sem).wait()

    @pl.loop(0, 6)
    def _(b):
        old = mine[:, b].reshape(3 * HALF, TILE)
        new = old - dot3((t_hi[...], t_lo[...]), (p_hi[b], p_lo[b]), nn)
        mine[:, b] = jnp.where(top, 0.0, new).reshape(3, HALF, TILE)

        @pl.when((b == 0) & (z < 2))
        def _():
            panel = jnp.where(z == 0, c_all[:, :TILE], c_all[:, TILE:])
            above = top & (row * TILE + core * HALF + sub < z * TILE + lane)
            mine[:, 0] = jnp.where(above, 0.0, panel).reshape(3, HALF, TILE)
        put(b).start()

    def left_for(whole, send):
        remote(whole, whole, send, b_recv, partner).wait_send()

    @pl.when(core == 1)
    def _():
        for src_row in range(2):
            for q in range(4):
                kids, _ = c_tree(src_row, q)
                whole = pct.at[src_row, :, pl.ds(q * (TILE // 4), TILE // 4), :]
                for m, (_, cond) in enumerate(kids):
                    @pl.when(cond)
                    def _():
                        left_for(whole, c_send.at[src_row, q, m])
        for c in range(2):
            for way in range(2):
                kids, _ = r_tree(c, way)
                @pl.when(kids[0][1])
                def _():
                    left_for(rp.at[c, :, pl.ds(way * NB, NB), :], r_send.at[c, way])
        left_for(pct, k_send.at[0])
        left_for(rp.at[:, :, pl.ds(0, NB), :], k_send.at[1])

    @pl.when(core == 0)
    def _():
        @pl.when(trees[0][0])
        def _():
            for n in range(len(z_kids)):
                left_for(s.at[pl.ds(0, NB), pl.ds(0, NB)], b_send.at[n])
        for group, (sy, sz) in zip(outs, ((0, 0), (1, 0), (1, 1))):
            @pl.when((x == 0) & (y == sy) & (z == sz))
            def _():
                left_for(s.at[pl.ds(0, NB), pl.ds(0, len(group) * NB)], a_send.at[0])
        for n in range(9):
            @pl.when(d_roles(n)[1])
            def _():
                left_for(s.at[pl.ds(0, 2 * NB), :], a_send.at[1])
        all_pieces = pct.at[0, pl.ds(0, 5), pl.ds(0, NB), :]
        slot = 0
        for cond, kids in trees[1:]:
            @pl.when(cond)
            def _():
                for n in range(len(kids)):
                    left_for(all_pieces, p_send.at[slot + n])
            slot += len(kids)
        left_for(all_pieces, p_send.at[slot])

    pltpu.make_async_copy(mine, mine, out_sem).wait()


def on_device(covariance):
    dma = pltpu.SemaphoreType.DMA
    n_c = TILE // 4 // CCH * 6
    n_r = NB // CCH * 3
    return pl.pallas_call(
        panel_kernel,
        out_shape=jax.ShapeDtypeStruct((3, 1, 6, 1, HALF, TILE), F32),
        in_specs=[pl.BlockSpec(memory_space=pltpu.HBM)],
        out_specs=pl.BlockSpec(memory_space=pl.ANY),
        scratch_shapes=[
            pltpu.VMEM((2, 6, TILE, TILE), F32),
            pltpu.VMEM((2, 3, TILE, TILE), F32),
            pltpu.VMEM((PANEL, PANEL), F32),
            pltpu.VMEM((PANEL, PANEL), F32),
            pltpu.VMEM((3, 6, HALF, TILE), F32),
            pltpu.VMEM((3 * HALF, PANEL), F32),
            pltpu.VMEM((3 * HALF, 3 * NB), F32),
            pltpu.VMEM((NB, 3 * NB), F32),
            pltpu.VMEM((3 * HALF, PANEL), BF16),
            pltpu.VMEM((3 * HALF, PANEL), BF16),
            pltpu.VMEM((6, PANEL, TILE), BF16),
            pltpu.VMEM((6, PANEL, TILE), BF16),
            dma, dma((3,)), dma, dma((2, 4, n_c)), dma((2, 2, n_r)), dma((10,)), dma((2, 4, 2)), dma((2, 3)), dma((10,)),
            dma((7,)), dma((2,)), dma((2, 4, 2)), dma((2, 2)), dma((2,)), dma((7,)), dma, dma, dma, dma, dma,
        ],
        compiler_params=pltpu.CompilerParams(collective_id=0, has_side_effects=True, vmem_limit_bytes=48 * 1024 * 1024),
        name="panel_step",
    )(covariance)


def solution(mesh):
    return jax.shard_map(
        on_device,
        mesh=mesh,
        in_specs=(P(None, "row", None, "col", None, None),),
        out_specs=P(None, "row", None, "col", "depth", None),
        check_vma=False,
    )
```

```python
import functools

import jax
import jax.numpy as jnp
from jax import lax
from jax.experimental import pallas as pl
from jax.experimental.pallas import tpu as pltpu
from jax.sharding import PartitionSpec as P

TILE = 256
PANEL = 512
NB = 128
NX = NY = 4
NZ = 8
CCH = 64
LAG = 3
TURNS = 6 * (TILE // 4 // CCH) + LAG * 7
HALF = TILE // 2
MESH = pl.DeviceIdType.MESH
F32 = jnp.float32
BF16 = jnp.bfloat16


def split(x):
    hi = x.astype(BF16)
    return hi, (x - hi.astype(F32)).astype(BF16)


def dot3(a, b, dims):
    (ah, al), (bh, bl) = a, b
    dot = functools.partial(lax.dot_general, dimension_numbers=(dims, ((), ())), preferred_element_type=F32)
    return dot(ah, bh) + (dot(ah, bl) + dot(al, bh))


def dot_nn(a, b):
    return dot3(split(a), split(b), ((1,), (0,)))


def lane_copy(v, k):
    return jnp.broadcast_to(v[:, k : k + 1], (8, NB))


def row_copy(v, k):
    return jnp.broadcast_to(v[k : k + 1, :], (8, NB))


def inverse_factor(rows):
    rows = list(rows)
    lane = lax.broadcasted_iota(jnp.int32, (8, NB), 1)
    sub = lax.broadcasted_iota(jnp.int32, (8, NB), 0)
    out = []
    for b in range(16):
        base = 8 * b
        cols = [[lane_copy(rows[i], base + k) for k in range(8)] for i in range(b, 16)]
        inside = (lane >= base) & (lane < base + 8)
        cur = jnp.where(inside, jnp.where(lane == sub + base, 1.0, 0.0), rows[b])
        diag = cols[0]
        scaled = jnp.zeros((8, NB), F32)
        for k in range(8):
            d = row_copy(diag[k], k)
            r = 1.0 / d
            scaled = jnp.where(sub == k, cur * lax.rsqrt(d), scaled)
            less = jnp.where(sub == k, diag[k] - 1.0, diag[k])
            for j in range(k + 1, 8):
                diag[j] = diag[j] - less * (row_copy(diag[k], j) * r)
            cur = cur - less * (row_copy(cur, k) * r)
        for i in range(b + 1, 16):
            acc = jnp.where(inside, 0.0, rows[i])
            for j in range(8):
                acc = acc - cols[i - b][j] * row_copy(cur, j)
            rows[i] = acc
        out.append(jnp.where(lane < base + 8, scaled, 0.0))
    return out


def panel_kernel(
    cov, out, pct, rp, s, w, mine, c_all, t_all, m3, t_hi, t_lo, p_hi, p_lo,
    b_recv, d_recv, a_recv, c_recv, r_recv, p_recv, c_core, r_core, p_core,
    b_send, a_send, c_send, r_send, k_send, p_send, in_sem, out_sem, local_sem, rows_sem, cols_sem,
):
    row = lax.axis_index("row")
    z = lax.axis_index("col")
    core = lax.axis_index("depth")
    x, y = row // NY, row % NY

    def at(xx, yy, zz, cc):
        return {"row": lax.rem(xx + NX, NX) * NY + lax.rem(yy + NY, NY), "col": lax.rem(zz + NZ, NZ), "depth": cc}

    def remote(src, dst, send, recv, to):
        return pltpu.make_async_remote_copy(src, dst, send, recv, device_id=to, device_id_type=MESH)

    partner = {"row": row, "col": z, "depth": 1 - core}
    links = [
        at(x + 1, y, z, 1), at(x - 1, y, z, 1), at(x, y + 1, z, 1),
        at(x, y - 1, z, 1), at(x, y, z + 1, 1), at(x, y, z - 1, 1),
    ]
    z_kids = [at(x, y, z + n, 0) for n in (4, 5, 3, 6, 2, 7, 1)]
    y_kids = [at(x, y + n, z, 0) for n in (2, 1, 3)]
    x_kids = [at(x + n, y, z, 0) for n in (2, 1, 3)]
    hub = row == 0
    trees = [(hub & (z == 0), z_kids), (hub, y_kids), (x == 0, x_kids)]

    own = [
        pltpu.make_async_copy(cov.at[:, 0, b, 0, pl.ds(core * HALF, HALF), :], mine.at[:, b], in_sem)
        for b in range(6)
    ]

    blocks = [
        (1, 0, 1, 0), (1, 1, 3, 0), (2, 0, 0, 1), (2, 1, 1, 1), (2, 2, 0, 1),
        (3, 0, 3, 1), (3, 1, 0, 2), (3, 2, 1, 1), (3, 3, 3, 1),
    ]

    def d_place(n):
        i, j, _, _ = blocks[n]
        return s.at[pl.ds(i * NB, NB), pl.ds(j * NB, NB)]

    def d_input(n):
        i, j, _, _ = blocks[n]
        return cov.at[0, 0, 0, 0, pl.ds(i % 2 * NB, NB), pl.ds(j % 2 * NB, NB)]

    def d_roles(n):
        i, j, ax, ay = blocks[n]
        source = (x == 0) & (y == i // 2) & (z == j // 2)
        agent = (x == ax) & (y == ay) & (z == j // 2)
        return source, agent, (ax, ay) == (0, i // 2)

    hubs = [at(0 * x, 0 * y, n + 0 * z, 0) for n in (4, 5, 3, 6, 2, 7, 1, 0)]
    outs = [[n for n in range(9) if blocks[n][0] // 2 == sy and blocks[n][1] // 2 == sz and not d_roles(n)[2]] for sy, sz in ((0, 0), (1, 0), (1, 1))]
    d_rows = {1: s.at[pl.ds(0, NB), pl.ds(0, 2 * NB)], 2: s.at[pl.ds(0, NB), pl.ds(0, 3 * NB)], 3: s.at[pl.ds(0, NB), :]}

    barrier = pltpu.get_barrier_semaphore()
    pl.semaphore_signal(barrier, inc=1, device_id=partner, device_id_type=MESH)

    @pl.when(core == 1)
    def _():
        for link in links:
            pl.semaphore_signal(barrier, inc=1, device_id=link, device_id_type=MESH)
        pl.semaphore_wait(barrier, 7)

    @pl.when(core == 0)
    def _():
        @pl.when(x != 0)
        def _():
            pl.semaphore_signal(barrier, inc=1, device_id=at(0 * x, y, z, 0), device_id_type=MESH)
        @pl.when((x == 0) & (y != 0))
        def _():
            pl.semaphore_signal(barrier, inc=1, device_id=at(x, 0 * y, z, 0), device_id_type=MESH)
        @pl.when(hub & (z != 0))
        def _():
            pl.semaphore_signal(barrier, inc=1, device_id=at(x, y, 0 * z, 0), device_id_type=MESH)
        want = 1 + sum(cond.astype(jnp.int32) * len(kids) for cond, kids in trees)
        for n in range(9):
            i, j, ax, ay = blocks[n]
            source, agent, same = d_roles(n)
            @pl.when(hub)
            def _():
                to = at(0 * x + ax, 0 * y + ay, 0 * z + j // 2, 0)
                pl.semaphore_signal(barrier, inc=1, device_id=to, device_id_type=MESH)
            want += agent.astype(jnp.int32) * 8
            if not same:
                @pl.when(agent)
                def _():
                    to = at(0 * x, 0 * y + i // 2, z, 0)
                    pl.semaphore_signal(barrier, inc=1, device_id=to, device_id_type=MESH)
                want += source.astype(jnp.int32)
        pl.semaphore_wait(barrier, want)

    @pl.when(core == 0)
    def _():
        for n in range(9):
            i, j, ax, ay = blocks[n]
            source, agent, same = d_roles(n)
            if not same:
                @pl.when(source)
                def _():
                    to = at(0 * x + ax, 0 * y + ay, z, 0)
                    remote(d_input(n), d_place(n), a_send.at[0], a_recv, to).start()
        for n in range(9):
            i, j, ax, ay = blocks[n]
            source, agent, same = d_roles(n)
            @pl.when(agent)
            def _():
                if not same:
                    remote(d_place(n), d_place(n), a_send.at[0], a_recv, partner).wait_recv()
                for to in hubs:
                    remote(d_input(n) if same else d_place(n), d_place(n), a_send.at[1], d_recv.at[i - 1], to).start()

    def c_tree(src, q):
        dx, dy = x, lax.rem(y - src + NY, NY)
        if q % 2:
            dx, dy = lax.rem(NX - dx, NX), lax.rem(NY - dy, NY)
        if q >= 2:
            dx, dy = dy, dx
        along = (dy == 0) & (dx <= 2) | (dx == 3) & (dy >= 1)
        across = (dx >= 1) & (dy <= 2)
        hops = jnp.where((dx == 0) & (dy > 0), dy + 4, dx + dy)
        one, two = (q % 2, 2 + q % 2) if q < 2 else (2 + q % 2, q % 2)
        return [(one, along), (two, across)], hops

    def r_tree(c, way):
        hops = lax.rem((z - c if way == 0 else c - z) + NZ, NZ)
        return [(4 + way, hops <= 6)], hops

    def pass_on(live, src, dst, here, kids, sends, recv, to_core):
        def forward(ref):
            for n, (link, cond) in enumerate(kids):
                @pl.when(cond)
                def _():
                    remote(ref, dst, sends(n), recv, links[link]).start()
            to_core(ref)

        @pl.when(live & here)
        def _():
            forward(src)

        @pl.when(live & jnp.logical_not(here))
        def _():
            remote(dst, dst, sends(0), recv, partner).wait_recv()
            forward(dst)

    n_c = TILE // 4 // CCH * 6
    n_r = NB // CCH * 3

    pieces = [(0, 0), (1, 0), (2, 0), (1, 1), (2, 1), (3, 0), (3, 1), (2, 2), (3, 2), (3, 3)]

    def piece(k):
        i, j = pieces[k]
        return w.at[pl.ds(i * NB, NB), pl.ds(j * NB, NB)]

    def piece_value(i, j):
        return w[i * NB : (i + 1) * NB, j * NB : (j + 1) * NB]

    def hand_out(k):
        slot = 0
        for cond, kids in trees[1:]:
            @pl.when(cond)
            def _():
                for n, kid in enumerate(kids):
                    remote(piece(k), piece(k), p_send.at[slot + n], p_recv.at[k], kid).start()
            slot += len(kids)
        remote(piece(k), piece(k), p_send.at[slot], p_core.at[k], partner).start()

    def take(k):
        @pl.when(core == 1)
        def _():
            remote(piece(k), piece(k), p_send.at[0], p_core.at[k], partner).wait_recv()

        @pl.when((core == 0) & jnp.logical_not(hub))
        def _():
            remote(piece(k), piece(k), p_send.at[0], p_recv.at[k], partner).wait_recv()
            hand_out(k)

    own_rows = (x == 0) & (y <= 1) & (core == 1)
    own_cols = (z <= 1) & (core == 1)

    @pl.when(own_rows)
    def _():
        for b in range(6):
            pltpu.make_async_copy(cov.at[0, 0, b, 0], pct.at[y, b], rows_sem).start()

    @pl.when(own_cols)
    def _():
        for a in range(3):
            pltpu.make_async_copy(cov.at[a, 0, 0, 0], rp.at[z, a], cols_sem).start()

    @pl.when(core == 1)
    def _():
        @pl.loop(0, TURNS)
        def _(g):
            for q in range(4):
                for src_row in range(2):
                    kids, hops = c_tree(src_row, q)
                    i = g - LAG * hops
                    live = (i >= 0) & (i < n_c)
                    i = jnp.clip(i, 0, n_c - 1)
                    per = n_c // 6
                    b = i // per
                    rows = pl.ds(pl.multiple_of(q * (TILE // 4) + i % per * CCH, CCH), CCH)
                    src = cov.at[0, 0, b, 0, rows, :]
                    dst = pct.at[src_row, b, rows, :]
                    def to_core(ref):
                        for h in range(2):
                            @pl.when(i == n_c // 2 * (h + 1) - 1)
                            def _():
                                part = pl.ds(3 * h, 3), 0, pl.ds(q * (TILE // 4), TILE // 4)
                                home = pct.at[src_row, part[0], part[2], :]
                                @pl.when(hops == 0)
                                def _():
                                    remote(cov.at[0, 0, part[0], 0, part[2], :], home, k_send.at[0], c_core.at[src_row, q, h], partner).start()
                                @pl.when(hops != 0)
                                def _():
                                    remote(home, home, k_send.at[0], c_core.at[src_row, q, h], partner).start()
                    pass_on(live, src, dst, hops == 0, kids, lambda m: c_send.at[src_row, q, m], c_recv.at[src_row, q, i], to_core)
            for way in range(2):
                for c in range(2):
                    kids, hops = r_tree(c, way)
                    i = g - LAG * hops
                    live = (i >= 0) & (i < n_r)
                    i = jnp.clip(i, 0, n_r - 1)
                    per = n_r // 3
                    a = i // per
                    rows = pl.ds(pl.multiple_of(way * NB + i % per * CCH, CCH), CCH)
                    src = cov.at[a, 0, 0, 0, rows, :]
                    dst = rp.at[c, a, rows, :]
                    def to_core(ref):
                        if way == 0:
                            @pl.when(i % (n_r // 3) == n_r // 3 - 1)
                            def _():
                                home = rp.at[c, a, pl.ds(0, NB), :]
                                @pl.when(hops == 0)
                                def _():
                                    remote(cov.at[a, 0, 0, 0, pl.ds(0, NB), :], home, k_send.at[1], r_core.at[c, a], partner).start()
                                @pl.when(hops != 0)
                                def _():
                                    remote(home, home, k_send.at[1], r_core.at[c, a], partner).start()
                    pass_on(live, src, dst, hops == 0, kids, lambda m: r_send.at[c, way], r_recv.at[c, way, i], to_core)

        for copy in own:
            copy.start()

    @pl.when((core == 0) & jnp.logical_not(hub))
    def _():
        for copy in own:
            copy.start()

    @pl.when((core == 0) & hub)
    def _():
        first = s.at[pl.ds(0, NB), pl.ds(0, NB)]
        first_in = cov.at[0, 0, 0, 0, pl.ds(0, NB), pl.ds(0, NB)]

        @pl.when(z == 0)
        def _():
            for n, kid in enumerate(z_kids):
                remote(first_in, first, b_send.at[n], b_recv, kid).start()
            copy = pltpu.make_async_copy(first_in, first, local_sem)
            copy.start()
            copy.wait()
        @pl.when(z != 0)
        def _():
            remote(first, first, b_send.at[0], b_recv, partner).wait_recv()

        def block(i, j):
            return s[i * NB : (i + 1) * NB, j * NB : (j + 1) * NB]

        def wait_row(i):
            remote(d_rows[i], d_rows[i], b_send.at[0], d_recv.at[i - 1], partner).wait_recv()

        low = {}
        inv = {}

        def publish(i, j, value):
            w[i * NB : (i + 1) * NB, j * NB : (j + 1) * NB] = value
            hand_out(pieces.index((i, j)))

        def product(a, b):
            return dot3(a, b, ((1,), (1,)))

        def solve(i, j):
            rest = block(i, j)
            for n in range(j):
                rest = rest - product(low[i, n], low[j, n])
            got = product(split(rest), inv[j])
            low[i, j] = split(got)
            publish(i, j, got)

        for k in range(4):
            if k == 1:
                wait_row(1)
            if k > 0:
                solve(k, k - 1)
            piv = block(k, k)
            for j in range(k):
                piv = piv - product(low[k, j], low[k, j])
            if 0 < k < 3:
                wait_row(k + 1)
                for j in range(k):
                    solve(k + 1, j)
            wk = jnp.concatenate(inverse_factor([piv[8 * i : 8 * i + 8] for i in range(16)]), axis=0)
            publish(k, k, wk)
            inv[k] = split(wk)
            if k == 0:
                for copy in own:
                    copy.start()

    late = len(pieces) - 2
    last = len(pieces) - 1
    for k in range(late):
        take(k)
    nt, nn = ((1,), (1,)), ((1,), (0,))

    inverse_rows = []
    for i in range(4):
        if i == 3:
            take(late)
        row_blocks = []
        for j in range(i):
            acc = None
            for n in range(j, i):
                part = dot_nn(piece_value(i, n), inverse_rows[n][:, j * NB : (j + 1) * NB])
                acc = part if acc is None else acc + part
            row_blocks.append(acc)
        if i == 0:
            inverse_rows.append(piece_value(0, 0))
        elif i < 3:
            left = -dot_nn(piece_value(i, i), jnp.concatenate(row_blocks, axis=1))
            inverse_rows.append(jnp.concatenate([left, piece_value(i, i)], axis=1))
        else:
            m3[...] = jnp.concatenate(row_blocks, axis=1)
    tri = [split(v) for v in inverse_rows]

    passes_on = (core == 0) & (x == 0)

    @pl.when(passes_on)
    def _():
        take(last)

    @pl.when(core == 0)
    def _():
        for q in range(4):
            for src_row in range(2):
                for h in range(2):
                    dst = pct.at[src_row, pl.ds(3 * h, 3), pl.ds(q * (TILE // 4), TILE // 4), :]
                    remote(dst, dst, b_send.at[0], c_core.at[src_row, q, h], partner).wait_recv()
        for c in range(2):
            for a in range(3):
                dst = rp.at[c, a, pl.ds(0, NB), :]
                remote(dst, dst, b_send.at[0], r_core.at[c, a], partner).wait_recv()

    @pl.when(own_rows)
    def _():
        pltpu.make_async_copy(pct.at[y], pct.at[y], rows_sem).wait()

    @pl.when(own_cols)
    def _():
        pltpu.make_async_copy(rp.at[z], rp.at[z], cols_sem).wait()

    rows = [rp[c, :, pl.ds(core * HALF, HALF), :].reshape(3 * HALF, TILE) for c in range(2)]
    r_hi, r_lo = split(jnp.concatenate(rows, axis=1))
    c_parts = []
    for j in range(3):
        e = (j + 1) * NB
        got = dot3((r_hi[:, :e], r_lo[:, :e]), tri[j], nt)
        c_all[:, j * NB : e] = got
        c_parts.append(split(got))
    for j in range(3):
        cols = slice(j * NB, (j + 1) * NB)
        lhs = [jnp.concatenate([c_parts[i][h] for i in range(j, 3)], axis=1) for h in range(2)]
        rhs = [jnp.concatenate([tri[i][h][:, cols] for i in range(j, 3)], axis=0) for h in range(2)]
        t_all[:, cols] = dot3(lhs, rhs, nn)

    @pl.loop(0, 6)
    def _(b):
        for c in range(2):
            hi, lo = split(pct[c, b])
            p_hi[b, c * TILE : (c + 1) * TILE] = hi
            p_lo[b, c * TILE : (c + 1) * TILE] = lo

    @pl.when(jnp.logical_not(passes_on))
    def _():
        take(last)

    left = -dot_nn(piece_value(3, 3), m3[...])
    end = split(jnp.concatenate([left, piece_value(3, 3)], axis=1))
    c_last = dot3((r_hi, r_lo), end, nt)
    c_all[:, 3 * NB :] = c_last
    t_last = dot3(split(c_last), end, nn)
    hi, lo = split(t_all[...] + t_last[:, : 3 * NB])
    t_hi[:, : 3 * NB] = hi
    t_lo[:, : 3 * NB] = lo
    hi, lo = split(t_last[:, 3 * NB :])
    t_hi[:, 3 * NB :] = hi
    t_lo[:, 3 * NB :] = lo

    sub = lax.broadcasted_iota(jnp.int32, (3 * HALF, TILE), 0)
    lane = lax.broadcasted_iota(jnp.int32, (3 * HALF, TILE), 1)
    top = (sub < HALF) & (row < 2)

    def put(b):
        return pltpu.make_async_copy(mine.at[:, b], out.at[:, 0, b, 0], out_sem)

    pltpu.make_async_copy(mine, mine, in_sem).wait()

    @pl.loop(0, 6)
    def _(b):
        old = mine[:, b].reshape(3 * HALF, TILE)
        new = old - dot3((t_hi[...], t_lo[...]), (p_hi[b], p_lo[b]), nn)
        mine[:, b] = jnp.where(top, 0.0, new).reshape(3, HALF, TILE)

        @pl.when((b == 0) & (z < 2))
        def _():
            panel = jnp.where(z == 0, c_all[:, :TILE], c_all[:, TILE:])
            above = top & (row * TILE + core * HALF + sub < z * TILE + lane)
            mine[:, 0] = jnp.where(above, 0.0, panel).reshape(3, HALF, TILE)
        put(b).start()

    def left_for(whole, send):
        remote(whole, whole, send, b_recv, partner).wait_send()

    @pl.when(core == 1)
    def _():
        for src_row in range(2):
            for q in range(4):
                kids, _ = c_tree(src_row, q)
                whole = pct.at[src_row, :, pl.ds(q * (TILE // 4), TILE // 4), :]
                for m, (_, cond) in enumerate(kids):
                    @pl.when(cond)
                    def _():
                        left_for(whole, c_send.at[src_row, q, m])
        for c in range(2):
            for way in range(2):
                kids, _ = r_tree(c, way)
                @pl.when(kids[0][1])
                def _():
                    left_for(rp.at[c, :, pl.ds(way * NB, NB), :], r_send.at[c, way])
        left_for(pct, k_send.at[0])
        left_for(rp.at[:, :, pl.ds(0, NB), :], k_send.at[1])

    @pl.when(core == 0)
    def _():
        @pl.when(trees[0][0])
        def _():
            for n in range(len(z_kids)):
                left_for(s.at[pl.ds(0, NB), pl.ds(0, NB)], b_send.at[n])
        for group, (sy, sz) in zip(outs, ((0, 0), (1, 0), (1, 1))):
            @pl.when((x == 0) & (y == sy) & (z == sz))
            def _():
                left_for(s.at[pl.ds(0, NB), pl.ds(0, len(group) * NB)], a_send.at[0])
        for n in range(9):
            @pl.when(d_roles(n)[1])
            def _():
                left_for(s.at[pl.ds(0, 2 * NB), :], a_send.at[1])
        all_pieces = pct.at[0, pl.ds(0, 5), pl.ds(0, NB), :]
        slot = 0
        for cond, kids in trees[1:]:
            @pl.when(cond)
            def _():
                for n in range(len(kids)):
                    left_for(all_pieces, p_send.at[slot + n])
            slot += len(kids)
        left_for(all_pieces, p_send.at[slot])

    pltpu.make_async_copy(mine, mine, out_sem).wait()


def on_device(covariance):
    dma = pltpu.SemaphoreType.DMA
    n_c = TILE // 4 // CCH * 6
    n_r = NB // CCH * 3
    return pl.pallas_call(
        panel_kernel,
        out_shape=jax.ShapeDtypeStruct((3, 1, 6, 1, HALF, TILE), F32),
        in_specs=[pl.BlockSpec(memory_space=pltpu.HBM)],
        out_specs=pl.BlockSpec(memory_space=pl.ANY),
        scratch_shapes=[
            pltpu.VMEM((2, 6, TILE, TILE), F32),
            pltpu.VMEM((2, 3, TILE, TILE), F32),
            pltpu.VMEM((PANEL, PANEL), F32),
            pltpu.VMEM((PANEL, PANEL), F32),
            pltpu.VMEM((3, 6, HALF, TILE), F32),
            pltpu.VMEM((3 * HALF, PANEL), F32),
            pltpu.VMEM((3 * HALF, 3 * NB), F32),
            pltpu.VMEM((NB, 3 * NB), F32),
            pltpu.VMEM((3 * HALF, PANEL), BF16),
            pltpu.VMEM((3 * HALF, PANEL), BF16),
            pltpu.VMEM((6, PANEL, TILE), BF16),
            pltpu.VMEM((6, PANEL, TILE), BF16),
            dma, dma((3,)), dma, dma((2, 4, n_c)), dma((2, 2, n_r)), dma((10,)), dma((2, 4, 2)), dma((2, 3)), dma((10,)),
            dma((7,)), dma((2,)), dma((2, 4, 2)), dma((2, 2)), dma((2,)), dma((7,)), dma, dma, dma, dma, dma,
        ],
        compiler_params=pltpu.CompilerParams(collective_id=0, has_side_effects=True, vmem_limit_bytes=48 * 1024 * 1024),
        name="panel_step",
    )(covariance)


def solution(mesh):
    return jax.shard_map(
        on_device,
        mesh=mesh,
        in_specs=(P(None, "row", None, "col", None, None),),
        out_specs=P(None, "row", None, "col", "depth", None),
        check_vma=False,
    )
```
